256 devices in a mesh: ctx: 64 (over x, z_hi, y), head: 4 (over z_lo, core).
Axes of the slice: x: 4, y: 4, z: 8 (z_hi: 4, z_lo: 2; z = z_hi * 2 + z_lo), core: 2. Of those that a mesh axis runs over, the one named last changes fastest.
Arguments:
- hidden_in: bfloat16 [2, 32768, 2048], P(None, 'ctx', 'head'), may hold values from -6 to 6
- projected: bfloat16 [3, 2, 32768, 2048], P(None, None, 'ctx', 'head'), may hold values from -4.5 to 4.5
- w_out: bfloat16 [2048, 2048], P(None, 'head'), may hold values from -0.125 to 0.125
- fast_up: bfloat16 [2, 4, 512, 512], P(None, 'head'), may hold values from -0.25 to 0.25
- fast_down: bfloat16 [4, 512, 512], P('head'), may hold values from -0.25 to 0.25
- learn_rates: float32 [4, 2, 32768], P('head', None, 'ctx'), may hold values from 0.02 to 0.2
Outputs:
- layer_out: bfloat16 [2, 32768, 2048], P(None, 'ctx', 'head')
- fast_up_final: float32 [2, 4, 512, 512], P(None, 'head')
- fast_down_final: float32 [4, 512, 512], P('head')
The draws below stay inside these ranges and needn't reach their ends.
All inputs are finite; a program needn't handle non-finite values.
Results may differ from the reference program's by a relative error of at most 0.0087.
Values may be sent and summed in bfloat16 or wider, within the bound.
A program may use at most 128 MiB of HBM per device.

```python
import math
import jax
import jax.numpy as jnp
from jax import lax

D = 2048
HA = 16
HD = 128
HF = 4
FD = 512
FH = 512
WIN = 512
BLOCKS = 2
BLOCK_LEN = 32768


def draw_projected(key, part):
    base_key = jax.random.fold_in(jax.random.fold_in(key, 7), 0)
    full_shape = (3, BLOCKS, BLOCK_LEN, D)
    base_draw = jnp.clip(jax.random.normal(base_key, full_shape, jnp.float32), -4.5, 4.5)
    return base_draw.astype(jnp.bfloat16)


def steps_of(key, shape, shards, low, top_value):
    def one(dim, parts):
        draws = jax.random.uniform(jax.random.fold_in(jax.random.fold_in(key, 6), dim), (parts,), jnp.float32, low / len(shards), top_value / len(shards))
        return jnp.repeat(jnp.exp(draws), shape[dim] // parts).reshape((-1,) + (1,) * (len(shape) - dim - 1))

    loudness = one(*shards[0])
    for cut in shards[1:]:
        loudness = loudness * one(*cut)
    return loudness


def centred(own_key, dims, spread, bound, shards=(), kind=jnp.bfloat16):
    array = spread * jax.random.normal(own_key, dims, jnp.float32)
    if shards:
        array = array * steps_of(own_key, dims, shards, -0.22, 0.18)
    return jnp.clip(array, -bound, bound).astype(kind)


def setup_inputs(seed: int = 0) -> dict:
    arg_keys = jax.random.split(jax.random.key(seed), 7)
    return {
        "hidden_in": centred(arg_keys[0], (BLOCKS, BLOCK_LEN, D), 1.0, 6.0, ((1, 64), (2, 4))),
        "projected": draw_projected(jax.random.fold_in(arg_keys[6], 71), 0),
        "w_out": centred(arg_keys[2], (D, D), D ** -0.5, 0.125, ((1, 4),)),
        "fast_up": centred(arg_keys[3], (2, HF, FD, FH), FD ** -0.5, 0.25, ((1, 4),)),
        "fast_down": centred(arg_keys[4], (HF, FH, FD), FH ** -0.5, 0.25, ((0, 4),)),
        "learn_rates": jnp.clip(jnp.exp(math.log(0.2) - 2.3025851 * jax.random.uniform(arg_keys[5], (HF, BLOCKS, BLOCK_LEN), jnp.float32) ** steps_of(arg_keys[5], (HF, BLOCKS, BLOCK_LEN), ((0, 4), (2, 64)), -0.2, 0.2)), 0.02, 0.2),
    }


def attention(projected):
    seq_len = BLOCKS * BLOCK_LEN
    queries = projected[0].reshape(seq_len, HA, HD)
    key_rows = projected[1].reshape(seq_len, HA, HD)
    value_rows = projected[2].reshape(seq_len, HA, HD)
    padding = jnp.zeros((WIN, HA, HD), jnp.bfloat16)
    key_padded = jnp.concatenate([padding, key_rows], axis=0)
    value_padded = jnp.concatenate([padding, value_rows], axis=0)
    score_scale = 1.0 / math.sqrt(HD)
    row_ids = jnp.arange(WIN, dtype=jnp.int32)[:, None]
    col_ids = jnp.arange(2 * WIN, dtype=jnp.int32)[None, :]
    distance = row_ids + WIN - col_ids

    def one_block(block_index):
        start_row = (block_index * WIN).astype(jnp.int32)
        query_block = lax.dynamic_slice_in_dim(queries, start_row, WIN, 0)
        key_block = lax.dynamic_slice_in_dim(key_padded, start_row, 2 * WIN, 0)
        value_block = lax.dynamic_slice_in_dim(value_padded, start_row, 2 * WIN, 0)
        scores = jnp.einsum('qhd,khd->hqk', query_block.astype(jnp.float32), key_block.astype(jnp.float32)) * score_scale
        allowed = (distance >= 0) & (distance < WIN) & (col_ids + start_row >= WIN)
        scores = jnp.where(allowed[None], scores, -1e+30)
        row_peak = lax.optimization_barrier(jnp.max(scores, axis=-1, keepdims=True))
        lifted = jnp.exp(scores - row_peak)
        weights = (lifted / lax.optimization_barrier(jnp.sum(lifted, axis=-1, keepdims=True))).astype(jnp.bfloat16)
        result = jnp.einsum('hqk,khd->qhd', weights.astype(jnp.float32), value_block.astype(jnp.float32))
        return result.astype(jnp.bfloat16).reshape(WIN, HA * HD)
    blocks_out = lax.map(one_block, jnp.arange(seq_len // WIN, dtype=jnp.int32))
    return blocks_out.reshape(BLOCKS, BLOCK_LEN, HA * HD)

def fast_apply(rows_in, w_one, w_three, w_two):
    pre_gate = jnp.dot(rows_in, w_one, preferred_element_type=jnp.float32)
    pre_up = jnp.dot(rows_in, w_three, preferred_element_type=jnp.float32)
    hidden = (pre_gate * jax.nn.sigmoid(pre_gate) * pre_up).astype(jnp.bfloat16)
    result = jnp.dot(hidden, w_two, preferred_element_type=jnp.float32)
    return result * lax.rsqrt(lax.optimization_barrier(jnp.mean(result * result, axis=-1, keepdims=True)) + 1e-05)

def fast_grads(key_rows, value_rows, step_size, w_one, w_three, w_two):
    pre_gate = jnp.dot(key_rows, w_one, preferred_element_type=jnp.float32)
    pre_up = jnp.dot(key_rows, w_three, preferred_element_type=jnp.float32)
    gate_sig = jax.nn.sigmoid(pre_gate)
    hidden = (pre_gate * gate_sig * pre_up).astype(jnp.bfloat16)
    out_grad = (-step_size[:, None] * value_rows.astype(jnp.float32)).astype(jnp.bfloat16)
    grad_two = jnp.dot(hidden.T, out_grad, preferred_element_type=jnp.float32)
    hidden_grad = jnp.dot(out_grad, w_two.T, preferred_element_type=jnp.float32)
    gate_grad = (hidden_grad * pre_up * gate_sig * (1.0 + pre_gate * (1.0 - gate_sig))).astype(jnp.bfloat16)
    up_grad = (hidden_grad * pre_gate * gate_sig).astype(jnp.bfloat16)
    grad_one = jnp.dot(key_rows.T, gate_grad, preferred_element_type=jnp.float32)
    grad_three = jnp.dot(key_rows.T, up_grad, preferred_element_type=jnp.float32)
    return (grad_one, grad_three, grad_two)

def renorm(old_weight, gradient):
    moved_weight = old_weight - gradient
    return moved_weight * (jnp.sqrt(jnp.sum(old_weight * old_weight)) / jnp.sqrt(jnp.sum(moved_weight * moved_weight) + 1e-06))

def reference(hidden_in, projected, w_out, fast_up, fast_down, learn_rates):
    attended = attention(projected)
    step_scale = 1.0 / math.sqrt(BLOCK_LEN)
    mixed_heads = []
    final_one = []
    final_three = []
    final_two = []
    for head_idx in range(HF):
        low = head_idx * FD
        high = low + FD
        weights_now = (fast_up[0, head_idx].astype(jnp.float32), fast_up[1, head_idx].astype(jnp.float32), fast_down[head_idx].astype(jnp.float32))
        pieces = []
        for block_idx in range(BLOCKS):
            w_one = weights_now[0].astype(jnp.bfloat16)
            w_three = weights_now[1].astype(jnp.bfloat16)
            w_two = weights_now[2].astype(jnp.bfloat16)
            fast_out = fast_apply(projected[0, block_idx, :, low:high], w_one, w_three, w_two)
            pieces.append((attended[block_idx, :, low:high].astype(jnp.float32) + fast_out).astype(jnp.bfloat16))
            gradients = fast_grads(projected[1, block_idx, :, low:high], projected[2, block_idx, :, low:high], learn_rates[head_idx, block_idx] * step_scale, w_one, w_three, w_two)
            weights_now = (renorm(weights_now[0], gradients[0]), renorm(weights_now[1], gradients[1]), renorm(weights_now[2], gradients[2]))
        mixed_heads.append(jnp.stack(pieces))
        final_one.append(weights_now[0])
        final_three.append(weights_now[1])
        final_two.append(weights_now[2])
    mixed = jnp.concatenate(mixed_heads, axis=2).reshape(BLOCKS * BLOCK_LEN, D)
    projected_out = jnp.dot(mixed, w_out, preferred_element_type=jnp.float32).reshape(BLOCKS, BLOCK_LEN, D)
    layer_out = (hidden_in.astype(jnp.float32) + projected_out).astype(jnp.bfloat16)
    fast_up_final = jnp.stack([jnp.stack(final_one), jnp.stack(final_three)])
    fast_down_final = jnp.stack(final_two)
    return (layer_out, fast_up_final, fast_down_final)
```

```python
import math

import jax
import jax.numpy as jnp
from jax import lax
from jax.experimental import pallas as pl
from jax.experimental.pallas import tpu as pltpu
from jax.sharding import PartitionSpec as P

MESH = pl.DeviceIdType.MESH
F32 = jnp.float32
BF16 = jnp.bfloat16
HD = 128
FD = 512
TOK = 512
HEADS = 4
BLOCKS = 2
BLOCK_LEN = 32768
LANES = 128
COLOURS = 4
SCALE = math.log2(math.e) / math.sqrt(HD)
ORDER = (
    ("x1", "x3", "y1", "y3"),
    ("x3", "x1", "y3", "y1"),
    ("y1", "y3", "x1", "x3"),
    ("y3", "y1", "x3", "x1"),
)


class Place:
    def __init__(self):
        ctx = lax.axis_index("ctx")
        self.head = lax.axis_index("head")
        self.x = ctx // 16
        self.z = (ctx // 4) % 4
        self.y = ctx % 4
        x_low, x_high = self.x % 2, self.x // 2
        y_low, y_high = self.y % 2, self.y // 2
        self.key = {
            "x1": (x_low + x_high) % 2,
            "x3": x_high,
            "y1": (y_low + y_high) % 2,
            "y3": y_high,
        }
        self.partner = {
            "x1": self.at(self.x + 1 - 2 * x_low, self.z, self.y),
            "x3": self.at(3 - self.x, self.z, self.y),
            "y1": self.at(self.x, self.z, self.y + 1 - 2 * y_low),
            "y3": self.at(self.x, self.z, 3 - self.y),
        }
        self.z_peer = [self.at(self.x, (self.z + d) % 4, self.y) for d in (1, 2, 3)]
        self.z_to = [(self.z + d) % 4 for d in (1, 2, 3)]
        self.before = ((ctx + 63) % 64, self.head)
        self.after = ((ctx + 1) % 64, self.head)
        self.sibling = self.head + 1 - 2 * (self.head % 2)
        self.across = (self.head + 2) % 4
        self.diagonal = (self.sibling + 2) % 4
        self.to_sibling = (ctx, self.sibling)
        self.to_across = (ctx, self.across)
        self.first = ctx == 0
        self.last = ctx // 63
        self.keep, self.send, self.mine = [], [], []
        for colour in range(COLOURS):
            keeps, sends, off = [], [], 0
            for step in range(4):
                length = 256 >> step
                key = self.key[ORDER[colour][step]]
                keeps.append(pl.multiple_of(off + key * length, 32))
                sends.append(pl.multiple_of(off + (1 - key) * length, 32))
                off = off + key * length
            self.keep.append(keeps)
            self.send.append(sends)
            self.mine.append(pl.multiple_of(off, 32))

    def at(self, x, z, y):
        return (x * 16 + z * 4 + y, self.head)

    def rows_of(self, colour):
        row = 0
        for which in range(COLOURS):
            row = row + jnp.where(colour == which, self.mine[which], 0)
        return pl.multiple_of(row, 32)


def remote(src, dst, send_sem, recv_sem, other):
    return pltpu.make_async_remote_copy(
        src_ref=src, dst_ref=dst, send_sem=send_sem, recv_sem=recv_sem, device_id=other, device_id_type=MESH
    )


def block_of(ref, matrix, row, length, colour):
    if isinstance(colour, int):
        lanes = pl.ds(colour * LANES, LANES)
    else:
        lanes = pl.ds(pl.multiple_of(colour * LANES, LANES), LANES)
    return ref.at[matrix, pl.ds(row, length), lanes]


def mm(a, b):
    return lax.dot_general(a, b, (((1,), (0,)), ((), ())), preferred_element_type=F32)


def mm_nt(a, b):
    return lax.dot_general(a, b, (((1,), (1,)), ((), ())), preferred_element_type=F32)


def mm_tn(a, b):
    return lax.dot_general(a, b, (((0,), (0,)), ((), ())), preferred_element_type=F32)


def square_sum(value):
    rows = jnp.sum(value * value, axis=0, keepdims=True)
    return jnp.sum(rows, axis=1, keepdims=True)


def layer_kernel(
    hidden_hbm, proj_hbm, wout_hbm, up_hbm, down_hbm, rates,
    out_hbm, moved_hbm, factor_out,
    proj, hidden, wout, state, q_land, o_out, o_land, stat_out, stat_land, attended, mixed, grad, total, moved0, moved1,
    land0, land1, land2, land3, z_land, piece, hid, gate_g, up_g, out_g, out_stage, out_acc,
    load_sem, store_sem, q_send, q_recv, o_send, o_recv, st_send, st_recv, h_send, h_recv,
    s_send, s_recv, z_send, z_recv, g_send, g_recv, zg_send, zg_recv,
):
    place = Place()
    lands = (land0, land1, land2, land3)
    moved = (moved0, moved1)

    loads = [
        pltpu.make_async_copy(proj_hbm.at[1, 0], proj.at[1, 0], load_sem.at[0]),
        pltpu.make_async_copy(proj_hbm.at[2, 0], proj.at[2, 0], load_sem.at[1]),
        pltpu.make_async_copy(up_hbm.at[0, 0], state.at[0], load_sem.at[2]),
        pltpu.make_async_copy(up_hbm.at[1, 0], state.at[1], load_sem.at[3]),
        pltpu.make_async_copy(down_hbm.at[0], state.at[2], load_sem.at[4]),
        pltpu.make_async_copy(proj_hbm.at[0], proj.at[0], load_sem.at[5]),
        pltpu.make_async_copy(proj_hbm.at[1, 1], proj.at[1, 1], load_sem.at[6]),
        pltpu.make_async_copy(proj_hbm.at[2, 1], proj.at[2, 1], load_sem.at[7]),
        pltpu.make_async_copy(wout_hbm, wout, load_sem.at[8]),
        pltpu.make_async_copy(hidden_hbm, hidden, load_sem.at[9]),
    ]
    for load in loads:
        load.start()

    barrier = pltpu.get_barrier_semaphore()
    others = list(place.partner.values()) + place.z_peer
    others += [place.before, place.after, place.to_sibling, place.to_across]
    for other in others:
        pl.semaphore_signal(barrier, inc=1, device_id=other, device_id_type=MESH)
    pl.semaphore_wait(barrier, len(others))

    def q_copy(block, head):
        lanes = pl.ds(head * HD, HD)
        sem = block * HEADS + head
        return remote(
            proj_hbm.at[0, block, :, lanes], q_land.at[block, :, lanes], q_send.at[sem], q_recv.at[sem], place.before
        )

    def o_copy(block, head):
        lanes = pl.ds(head * HD, HD)
        sem = block * HEADS + head
        return remote(
            o_out.at[block, :, lanes], o_land.at[block, :, lanes], o_send.at[sem], o_recv.at[sem], place.after
        )

    def stat_copy(block):
        return remote(stat_out.at[block], stat_land.at[block], st_send.at[block], st_recv.at[block], place.after)

    def head_copy(block, kind):
        owner, to = (
            (place.head, place.to_sibling),
            (place.head, place.to_across),
            (place.across, place.to_sibling),
        )[kind]
        rows = mixed.at[owner, block]
        return remote(rows, rows, h_send.at[block, kind], h_recv.at[block, kind], to)

    def scatter_copy(step, matrix, colour):
        length = 256 >> step
        return remote(
            block_of(grad, matrix, place.send[colour][step], length, colour),
            lands[step].at[matrix, colour],
            s_send.at[step, matrix, colour],
            s_recv.at[step, matrix, colour],
            place.partner[ORDER[colour][step]],
        )

    def z_copy(d, matrix):
        to = place.z_to[d]
        return remote(
            block_of(grad, matrix, place.rows_of(to), 32, to),
            z_land.at[d, matrix],
            z_send.at[d, matrix],
            z_recv.at[d, matrix],
            place.z_peer[d],
        )

    own_row = place.rows_of(place.z)

    def zg_copy(block, d, matrix):
        own = block_of(moved[block], matrix, own_row, 32, place.z)
        return remote(own, own, zg_send.at[d, matrix], zg_recv.at[d, matrix], place.z_peer[d])

    def gather_copy(block, step, matrix, colour):
        kept = block_of(moved[block], matrix, place.keep[colour][step], 256 >> step, colour)
        return remote(
            kept,
            kept,
            g_send.at[step, matrix, colour],
            g_recv.at[step, matrix, colour],
            place.partner[ORDER[colour][step]],
        )

    for block in range(BLOCKS):
        for head in range(HEADS):
            q_copy(block, head).start()

    def key_pass(block, weights, factors):
        step_scale = -1.0 / math.sqrt(BLOCK_LEN)

        def grown(value, which):
            return value if factors is None else value * factors[which]

        rows_per = 256
        for part in range(TOK // rows_per):
            rows = pl.ds(part * rows_per, rows_per)
            key = proj[1, block, rows, :]
            rate = rates[0, block : block + 1, part * rows_per : (part + 1) * rows_per] * step_scale
            rate = jnp.broadcast_to(rate, (LANES, rows_per)).T
            value = proj[2, block, rows, :].astype(F32)
            out_grad = (value * jnp.concatenate([rate] * 4, axis=1)).astype(BF16)
            out_g[rows, :] = out_grad
            gate = grown(mm(key, weights[0]), 0)
            up = grown(mm(key, weights[1]), 1)
            back = grown(mm_nt(out_grad, weights[2]), 2)
            sig = jax.nn.sigmoid(gate)
            gate_sig = gate * sig
            hid[rows, :] = (gate_sig * up).astype(BF16)
            gate_g[rows, :] = (back * up * (sig + gate_sig * (1.0 - sig))).astype(BF16)
            up_g[rows, :] = (back * gate_sig).astype(BF16)
        for matrix in (2, 1, 0):
            if matrix == 2:
                sums = mm_tn(hid[...], out_g[...])
            elif matrix == 1:
                sums = mm_tn(proj[1, block], up_g[...])
            else:
                sums = mm_tn(proj[1, block], gate_g[...])
            total[matrix] = sums
            grad[matrix] = sums.astype(BF16)
            for colour in range(COLOURS):
                scatter_copy(0, matrix, colour).start()

    def reduction(block, old_factors):
        for step in range(4):
            length = 256 >> step
            for matrix in (2, 1, 0):
                for colour in range(COLOURS):
                    scatter_copy(step, matrix, colour).wait_recv()
                    row = place.keep[colour][step]
                    kept = block_of(total, matrix, row, length, colour)
                    value = kept[...] + lands[step][matrix, colour].astype(F32)
                    kept[...] = value
                    block_of(grad, matrix, row, length, colour)[...] = value.astype(BF16)
                    if step < 3:
                        scatter_copy(step + 1, matrix, colour).start()
                if step == 3:
                    for d in range(3):
                        z_copy(d, matrix).start()
                yield
        for matrix in (2, 1, 0):
            value = block_of(total, matrix, own_row, 32, place.z)[...]
            for d in range(3):
                z_copy(d, matrix).wait_recv()
                value = value + z_land[d, matrix].astype(F32)
            if block == 0:
                value = block_of(state, matrix, own_row, 32, place.z)[...].astype(F32) - value
                piece[matrix] = value
            else:
                value = piece[matrix] * old_factors[matrix] - value
            block_of(moved[block], matrix, own_row, 32, place.z)[...] = value.astype(BF16)
            for d in range(3):
                zg_copy(block, d, matrix).start()
            yield
        for step in (3, 2, 1, 0):
            for matrix in (2, 1, 0):
                if step == 3:
                    for d in range(3):
                        zg_copy(block, d, matrix).wait_recv()
                for colour in range(COLOURS):
                    if step < 3:
                        gather_copy(block, step + 1, matrix, colour).wait_recv()
                    gather_copy(block, step, matrix, colour).start()
                yield
        for matrix in (2, 1, 0):
            for colour in range(COLOURS):
                gather_copy(block, 0, matrix, colour).wait_recv()
        for matrix in range(3):
            for colour in range(COLOURS):
                for step in range(4):
                    scatter_copy(step, matrix, colour).wait_send()
                    gather_copy(block, step, matrix, colour).wait_send()
            for d in range(3):
                z_copy(d, matrix).wait_send()
                zg_copy(block, d, matrix).wait_send()

    tile_row = lax.broadcasted_iota(jnp.int32, (HD, HD), 0)
    tile_col = lax.broadcasted_iota(jnp.int32, (HD, HD), 1)

    def softmax_part(scores, values):
        peak = jnp.max(scores, axis=1, keepdims=True)
        lifted = jnp.exp2((scores - peak) * SCALE)
        weight = jnp.sum(lifted, axis=1, keepdims=True)
        return mm(lifted.astype(BF16), values), peak * SCALE, weight

    def masked(scores, keep, last):
        width = scores.shape[1]
        if width == HD:
            return jnp.where(keep, scores, -1e30)
        if last:
            return jnp.concatenate([scores[:, : width - HD], jnp.where(keep, scores[:, width - HD :], -1e30)], axis=1)
        return jnp.concatenate([jnp.where(keep, scores[:, :HD], -1e30), scores[:, HD:]], axis=1)

    def far_item(block, head):
        lanes = pl.ds(head * HD, HD)
        q_copy(block, head).wait_recv()
        source = jnp.maximum(block - place.last, 0)
        for tile in range(4):
            rows = pl.ds(tile * HD, HD)
            span = pl.ds(tile * HD, TOK - tile * HD)
            scores = mm_nt(q_land[block, rows, lanes], proj[1, source, span, lanes])
            scores = masked(scores, tile_col > tile_row, False)
            result, peak, weight = softmax_part(scores, proj[2, source, span, lanes])
            o_out[block, rows, lanes] = (result / weight).astype(BF16)
            log_sum = jnp.broadcast_to(peak + jnp.log2(weight), (HD, LANES)).T
            stat_out[block, head : head + 1, rows] = log_sum[:1]
        o_copy(block, head).start()
        if head == HEADS - 1:
            stat_copy(block).start()

    def near_item(block, head):
        lanes = pl.ds(head * HD, HD)
        o_copy(block, head).wait_recv()
        if head == 0:
            stat_copy(block).wait_recv()
        for tile in range(4):
            rows = pl.ds(tile * HD, HD)
            span = pl.ds(0, (tile + 1) * HD)
            scores = mm_nt(proj[0, block, rows, lanes], proj[1, block, span, lanes])
            scores = masked(scores, tile_col <= tile_row, True)
            result, peak, weight = softmax_part(scores, proj[2, block, span, lanes])
            far_log = jnp.broadcast_to(stat_land[block, head : head + 1, rows], (LANES, HD)).T
            if block == 0:
                far_log = jnp.where(place.first, -1e30, far_log)
            top = jnp.maximum(peak, far_log)
            near_w = jnp.exp2(peak - top)
            far_w = jnp.exp2(far_log - top)
            far = o_land[block, rows, lanes].astype(F32)
            merged = (result * near_w + far * far_w) / (weight * near_w + far_w)
            attended[block, rows, lanes] = merged.astype(BF16)

    def query_part(block, weights, factors, part):
        rows = pl.ds(part * 256, 256)
        query = proj[0, block, rows, :]
        gate = mm(query, weights[0])
        up = mm(query, weights[1])
        if factors is not None:
            gate = gate * factors[0]
            up = up * factors[1]
        hidden_q = (gate * jax.nn.sigmoid(gate) * up).astype(BF16)
        result = mm(hidden_q, weights[2])
        if factors is not None:
            result = result * factors[2]
        fast = result * lax.rsqrt(jnp.mean(result * result, axis=1, keepdims=True) + 1e-05)
        mixed[place.head, block, rows, :] = (attended[block, rows, :].astype(F32) + fast).astype(BF16)

    def share(block):
        head_copy(block, 0).start()
        head_copy(block, 1).start()

    def forward(block):
        head_copy(block, 1).wait_recv()
        head_copy(block, 2).start()

    def project(block, turn):
        owner = (place.head, place.across, place.sibling, place.diagonal)[turn]
        if turn == 2:
            head_copy(block, 0).wait_recv()
        if turn == 3:
            head_copy(block, 2).wait_recv()
        product = mm(mixed[owner, block], wout[pl.ds(pl.multiple_of(owner * FD, FD), FD), :])
        if turn == 0:
            out_acc[...] = hidden[block].astype(F32) + product
        elif turn < 3:
            out_acc[...] += product
        else:
            out_stage[block] = (out_acc[...] + product).astype(BF16)
            pltpu.make_async_copy(out_stage.at[block], out_hbm.at[block], store_sem.at[block]).start()

    def run(steps, fillers, every):
        count, place_in = 0, 0
        for _ in steps:
            while place_in < len(fillers) and place_in < (count + 1) * every:
                fillers[place_in]()
                place_in += 1
            count += 1
        for filler in fillers[place_in:]:
            filler()

    for load in loads[:5]:
        load.wait()
    key_pass(0, [state[0], state[1], state[2]], None)
    for load in loads[5:]:
        load.wait()
    fillers = [lambda b=b, h=h: far_item(b, h) for b in range(BLOCKS) for h in range(HEADS)]
    fillers += [lambda h=h: near_item(0, h) for h in range(HEADS)]
    fillers += [lambda p=p: query_part(0, [state[0], state[1], state[2]], None, p) for p in range(2)]
    fillers += [lambda: share(0)]
    fillers += [lambda h=h: near_item(1, h) for h in range(HEADS)]
    run(reduction(0, None), fillers, 0.7)

    norm = []
    factors = []
    for matrix in range(3):
        first = jnp.sqrt(square_sum(state[matrix].astype(F32)))
        second = square_sum(moved0[matrix].astype(F32))
        factors.append(first * lax.rsqrt(second + 1e-06))
        norm.append(jnp.sqrt(second) * factors[matrix])
    key_pass(1, [moved0[0], moved0[1], moved0[2]], factors)
    fillers = [lambda p=p: query_part(1, [moved0[0], moved0[1], moved0[2]], factors, p) for p in range(2)]
    fillers += [lambda: share(1), lambda: forward(0)]
    fillers += [lambda t=t: project(0, t) for t in range(4)]
    fillers += [lambda: forward(1)]
    fillers += [lambda t=t: project(1, t) for t in range(4)]
    run(reduction(1, factors), fillers, 0.5)

    final = pltpu.make_async_copy(moved1, moved_hbm, store_sem.at[2])
    final.start()
    for matrix in range(3):
        last = square_sum(moved1[matrix].astype(F32))
        factor = norm[matrix] * lax.rsqrt(last + 1e-06)
        factor_out[matrix] = jnp.broadcast_to(factor, (8, LANES))
    for block in range(BLOCKS):
        for head in range(HEADS):
            q_copy(block, head).wait_send()
            o_copy(block, head).wait_send()
        stat_copy(block).wait_send()
        for kind in range(3):
            head_copy(block, kind).wait_send()
        pltpu.make_async_copy(out_stage.at[block], out_hbm.at[block], store_sem.at[block]).wait()
    final.wait()


def body(hidden_in, projected, w_out, fast_up, fast_down, learn_rates):
    dma = pltpu.SemaphoreType.DMA
    vmem = pltpu.VMEM
    hbm_spec = pl.BlockSpec(memory_space=pl.ANY)
    vmem_spec = pl.BlockSpec(memory_space=pltpu.VMEM)
    square = (FD, FD)
    layer_out, moved, factor = pl.pallas_call(
        layer_kernel,
        out_shape=(
            jax.ShapeDtypeStruct((BLOCKS, TOK, FD), BF16),
            jax.ShapeDtypeStruct((3, FD, FD), BF16),
            jax.ShapeDtypeStruct((3, 8, LANES), F32),
        ),
        in_specs=[hbm_spec] * 5 + [vmem_spec],
        out_specs=(hbm_spec, hbm_spec, vmem_spec),
        scratch_shapes=[
            vmem((3, BLOCKS, TOK, FD), BF16),
            vmem((BLOCKS, TOK, FD), BF16),
            vmem((4 * FD, FD), BF16),
            vmem((3,) + square, BF16),
            vmem((BLOCKS, TOK, FD), BF16),
            vmem((BLOCKS, TOK, FD), BF16),
            vmem((BLOCKS, TOK, FD), BF16),
            vmem((BLOCKS, 8, TOK), F32),
            vmem((BLOCKS, 8, TOK), F32),
            vmem((BLOCKS, TOK, FD), BF16),
            vmem((4, BLOCKS, TOK, FD), BF16),
            vmem((3,) + square, BF16),
            vmem((3,) + square, F32),
            vmem((3,) + square, BF16),
            vmem((3,) + square, BF16),
            vmem((3, COLOURS, 256, LANES), BF16),
            vmem((3, COLOURS, 128, LANES), BF16),
            vmem((3, COLOURS, 64, LANES), BF16),
            vmem((3, COLOURS, 32, LANES), BF16),
            vmem((3, 3, 32, LANES), BF16),
            vmem((3, 32, LANES), F32),
            vmem(square, BF16),
            vmem(square, BF16),
            vmem(square, BF16),
            vmem(square, BF16),
            vmem((BLOCKS, TOK, FD), BF16),
            vmem(square, F32),
            dma((10,)),
            dma((3,)),
            dma((8,)),
            dma((8,)),
            dma((8,)),
            dma((8,)),
            dma((2,)),
            dma((2,)),
            dma((2, 3)),
            dma((2, 3)),
            dma((4, 3, COLOURS)),
            dma((4, 3, COLOURS)),
            dma((3, 3)),
            dma((3, 3)),
            dma((4, 3, COLOURS)),
            dma((4, 3, COLOURS)),
            dma((3, 3)),
            dma((3, 3)),
        ],
        compiler_params=pltpu.CompilerParams(
            collective_id=0, has_side_effects=True, vmem_limit_bytes=60 << 20
        ),
    )(hidden_in, projected, w_out, fast_up, fast_down, learn_rates)
    finals = moved.astype(F32) * factor[:, :1, :1]
    return (layer_out, finals[:2, None], finals[2:])


def solution(mesh):
    in_specs = (
        P(None, "ctx", "head"),
        P(None, None, "ctx", "head"),
        P(None, "head"),
        P(None, "head", None, None),
        P("head", None, None),
        P("head", None, "ctx"),
    )
    out_specs = (P(None, "ctx", "head"), P(None, "head", None, None), P("head", None, None))
    return jax.shard_map(body, mesh=mesh, in_specs=in_specs, out_specs=out_specs, check_vma=False)
```

```python
import math

import jax
import jax.numpy as jnp
from jax import lax
from jax.experimental import pallas as pl
from jax.experimental.pallas import tpu as pltpu
from jax.sharding import PartitionSpec as P

MESH = pl.DeviceIdType.MESH
F32 = jnp.float32
BF16 = jnp.bfloat16
HD = 128
FD = 512
TOK = 512
HEADS = 4
BLOCKS = 2
BLOCK_LEN = 32768
LANES = 128
COLOURS = 4
SCALE = math.log2(math.e) / math.sqrt(HD)
ORDER = (
    ("x1", "x3", "y1", "y3"),
    ("x3", "x1", "y3", "y1"),
    ("y1", "y3", "x1", "x3"),
    ("y3", "y1", "x3", "x1"),
)


class Place:
    def __init__(self):
        ctx = lax.axis_index("ctx")
        self.head = lax.axis_index("head")
        self.x = ctx // 16
        self.z = (ctx // 4) % 4
        self.y = ctx % 4
        x_low, x_high = self.x % 2, self.x // 2
        y_low, y_high = self.y % 2, self.y // 2
        self.key = {
            "x1": (x_low + x_high) % 2,
            "x3": x_high,
            "y1": (y_low + y_high) % 2,
            "y3": y_high,
        }
        self.partner = {
            "x1": self.at(self.x + 1 - 2 * x_low, self.z, self.y),
            "x3": self.at(3 - self.x, self.z, self.y),
            "y1": self.at(self.x, self.z, self.y + 1 - 2 * y_low),
            "y3": self.at(self.x, self.z, 3 - self.y),
        }
        self.z_peer = [self.at(self.x, (self.z + d) % 4, self.y) for d in (1, 2, 3)]
        self.z_to = [(self.z + d) % 4 for d in (1, 2, 3)]
        self.before = ((ctx + 63) % 64, self.head)
        self.after = ((ctx + 1) % 64, self.head)
        self.sibling = self.head + 1 - 2 * (self.head % 2)
        self.across = (self.head + 2) % 4
        self.diagonal = (self.sibling + 2) % 4
        self.to_sibling = (ctx, self.sibling)
        self.to_across = (ctx, self.across)
        self.first = ctx == 0
        self.last = ctx // 63
        self.keep, self.send, self.mine = [], [], []
        for colour in range(COLOURS):
            keeps, sends, off = [], [], 0
            for step in range(4):
                length = 256 >> step
                key = self.key[ORDER[colour][step]]
                keeps.append(pl.multiple_of(off + key * length, 32))
                sends.append(pl.multiple_of(off + (1 - key) * length, 32))
                off = off + key * length
            self.keep.append(keeps)
            self.send.append(sends)
            self.mine.append(pl.multiple_of(off, 32))

    def at(self, x, z, y):
        return (x * 16 + z * 4 + y, self.head)

    def rows_of(self, colour):
        row = 0
        for which in range(COLOURS):
            row = row + jnp.where(colour == which, self.mine[which], 0)
        return pl.multiple_of(row, 32)


def remote(src, dst, send_sem, recv_sem, other):
    return pltpu.make_async_remote_copy(
        src_ref=src, dst_ref=dst, send_sem=send_sem, recv_sem=recv_sem, device_id=other, device_id_type=MESH
    )


def block_of(ref, matrix, row, length, colour):
    if isinstance(colour, int):
        lanes = pl.ds(colour * LANES, LANES)
    else:
        lanes = pl.ds(pl.multiple_of(colour * LANES, LANES), LANES)
    return ref.at[matrix, pl.ds(row, length), lanes]


def mm(a, b):
    return lax.dot_general(a, b, (((1,), (0,)), ((), ())), preferred_element_type=F32)


def mm_nt(a, b):
    return lax.dot_general(a, b, (((1,), (1,)), ((), ())), preferred_element_type=F32)


def mm_tn(a, b):
    return lax.dot_general(a, b, (((0,), (0,)), ((), ())), preferred_element_type=F32)


def square_sum(value):
    rows = jnp.sum(value * value, axis=0, keepdims=True)
    return jnp.sum(rows, axis=1, keepdims=True)


def layer_kernel(
    hidden_hbm, proj_hbm, wout_hbm, up_hbm, down_hbm, rates,
    out_hbm, up_out, down_out, factor_out,
    proj, hidden, wout, state, q_land, o_out, o_land, stat_out, stat_land, attended, mixed, grad, total, moved0, moved1,
    land0, land1, land2, land3, z_land, piece, hid, gate_g, up_g, out_g, out_stage, out_acc,
    load_sem, store_sem, q_send, q_recv, o_send, o_recv, st_send, st_recv, h_send, h_recv,
    s_send, s_recv, z_send, z_recv, g_send, g_recv, zg_send, zg_recv,
):
    place = Place()
    lands = (land0, land1, land2, land3)
    moved = (moved0, moved1)

    loads = [
        pltpu.make_async_copy(proj_hbm.at[1, 0], proj.at[1, 0], load_sem.at[0]),
        pltpu.make_async_copy(proj_hbm.at[2, 0], proj.at[2, 0], load_sem.at[1]),
        pltpu.make_async_copy(up_hbm.at[0, 0], state.at[0], load_sem.at[2]),
        pltpu.make_async_copy(up_hbm.at[1, 0], state.at[1], load_sem.at[3]),
        pltpu.make_async_copy(down_hbm.at[0], state.at[2], load_sem.at[4]),
        pltpu.make_async_copy(proj_hbm.at[0], proj.at[0], load_sem.at[5]),
        pltpu.make_async_copy(proj_hbm.at[1, 1], proj.at[1, 1], load_sem.at[6]),
        pltpu.make_async_copy(proj_hbm.at[2, 1], proj.at[2, 1], load_sem.at[7]),
        pltpu.make_async_copy(wout_hbm, wout, load_sem.at[8]),
        pltpu.make_async_copy(hidden_hbm, hidden, load_sem.at[9]),
    ]
    for load in loads:
        load.start()

    barrier = pltpu.get_barrier_semaphore()
    others = list(place.partner.values()) + place.z_peer
    others += [place.before, place.after, place.to_sibling, place.to_across]
    for other in others:
        pl.semaphore_signal(barrier, inc=1, device_id=other, device_id_type=MESH)
    pl.semaphore_wait(barrier, len(others))

    def q_copy(block, head, tile):
        lanes, rows = pl.ds(head * HD, HD), pl.ds(tile * HD, HD)
        sem = (block * HEADS + head) * 4 + tile
        return remote(
            proj_hbm.at[0, block, rows, lanes], q_land.at[block, rows, lanes], q_send.at[sem], q_recv.at[sem], place.before
        )

    def o_copy(block, head, tile):
        lanes, rows = pl.ds(head * HD, HD), pl.ds(tile * HD, HD)
        sem = (block * HEADS + head) * 4 + tile
        return remote(
            o_out.at[block, rows, lanes], o_land.at[block, rows, lanes], o_send.at[sem], o_recv.at[sem], place.after
        )

    def stat_copy(block):
        return remote(stat_out.at[block], stat_land.at[block], st_send.at[block], st_recv.at[block], place.after)

    def head_copy(block, kind):
        owner, to = (
            (place.head, place.to_sibling),
            (place.head, place.to_across),
            (place.across, place.to_sibling),
        )[kind]
        rows = mixed.at[owner, block]
        return remote(rows, rows, h_send.at[block, kind], h_recv.at[block, kind], to)

    def scatter_copy(step, matrix, colour):
        length = 256 >> step
        return remote(
            block_of(grad, matrix, place.send[colour][step], length, colour),
            lands[step].at[matrix, colour],
            s_send.at[step, matrix, colour],
            s_recv.at[step, matrix, colour],
            place.partner[ORDER[colour][step]],
        )

    def z_copy(d, matrix):
        to = place.z_to[d]
        return remote(
            block_of(grad, matrix, place.rows_of(to), 32, to),
            z_land.at[d, matrix],
            z_send.at[d, matrix],
            z_recv.at[d, matrix],
            place.z_peer[d],
        )

    own_row = place.rows_of(place.z)

    def zg_copy(block, d, matrix):
        own = block_of(moved[block], matrix, own_row, 32, place.z)
        return remote(own, own, zg_send.at[d, matrix], zg_recv.at[d, matrix], place.z_peer[d])

    def gather_copy(block, step, matrix, colour):
        kept = block_of(moved[block], matrix, place.keep[colour][step], 256 >> step, colour)
        return remote(
            kept,
            kept,
            g_send.at[step, matrix, colour],
            g_recv.at[step, matrix, colour],
            place.partner[ORDER[colour][step]],
        )

    q_copy(0, 0, 0).start()
    q_copy(0, 0, 1).start()
    q_copy(0, 0, 2).start()
    q_copy(0, 0, 3).start()
    q_copy(0, 1, 0).start()
    q_copy(0, 1, 1).start()
    q_copy(0, 1, 2).start()
    q_copy(0, 1, 3).start()

    def key_pass(block, weights, factors):
        step_scale = -1.0 / math.sqrt(BLOCK_LEN)

        def grown(value, which):
            return value if factors is None else value * factors[which]

        rows_per = 256
        for part in range(TOK // rows_per):
            rows = pl.ds(part * rows_per, rows_per)
            key = proj[1, block, rows, :]
            rate = rates[0, block : block + 1, part * rows_per : (part + 1) * rows_per] * step_scale
            rate = jnp.broadcast_to(rate, (LANES, rows_per)).T
            value = proj[2, block, rows, :].astype(F32)
            out_grad = (value * jnp.concatenate([rate] * 4, axis=1)).astype(BF16)
            out_g[rows, :] = out_grad
            gate = grown(mm(key, weights[0]), 0)
            up = grown(mm(key, weights[1]), 1)
            back = grown(mm_nt(out_grad, weights[2]), 2)
            sig = jax.nn.sigmoid(gate)
            gate_sig = gate * sig
            hid[rows, :] = (gate_sig * up).astype(BF16)
            gate_g[rows, :] = (back * up * (sig + gate_sig * (1.0 - sig))).astype(BF16)
            up_g[rows, :] = (back * gate_sig).astype(BF16)
        for matrix in (2, 1, 0):
            if matrix == 2:
                sums = mm_tn(hid[...], out_g[...])
            elif matrix == 1:
                sums = mm_tn(proj[1, block], up_g[...])
            else:
                sums = mm_tn(proj[1, block], gate_g[...])
            total[matrix] = sums
            grad[matrix] = sums.astype(BF16)
            for colour in range(COLOURS):
                scatter_copy(0, matrix, colour).start()

    def reduction(block, old_factors):
        for step in range(4):
            length = 256 >> step
            for matrix in (2, 1, 0):
                for colour in range(COLOURS):
                    scatter_copy(step, matrix, colour).wait_recv()
                    row = place.keep[colour][step]
                    kept = block_of(total, matrix, row, length, colour)
                    value = kept[...] + lands[step][matrix, colour].astype(F32)
                    kept[...] = value
                    block_of(grad, matrix, row, length, colour)[...] = value.astype(BF16)
                    if step < 3:
                        scatter_copy(step + 1, matrix, colour).start()
                if step == 3:
                    for d in range(3):
                        z_copy(d, matrix).start()
                yield
        for matrix in (2, 1, 0):
            value = block_of(total, matrix, own_row, 32, place.z)[...]
            for d in range(3):
                z_copy(d, matrix).wait_recv()
                value = value + z_land[d, matrix].astype(F32)
            if block == 0:
                value = block_of(state, matrix, own_row, 32, place.z)[...].astype(F32) - value
                piece[matrix] = value
            else:
                value = piece[matrix] * old_factors[matrix] - value
            block_of(moved[block], matrix, own_row, 32, place.z)[...] = value.astype(BF16)
            for d in range(3):
                zg_copy(block, d, matrix).start()
            yield
        for step in (3, 2, 1, 0):
            for matrix in (2, 1, 0):
                if step == 3:
                    for d in range(3):
                        zg_copy(block, d, matrix).wait_recv()
                for colour in range(COLOURS):
                    if step < 3:
                        gather_copy(block, step + 1, matrix, colour).wait_recv()
                    gather_copy(block, step, matrix, colour).start()
                yield
        for matrix in (2, 1, 0):
            for colour in range(COLOURS):
                gather_copy(block, 0, matrix, colour).wait_recv()
        for matrix in range(3):
            for colour in range(COLOURS):
                for step in range(4):
                    scatter_copy(step, matrix, colour).wait_send()
                    gather_copy(block, step, matrix, colour).wait_send()
            for d in range(3):
                z_copy(d, matrix).wait_send()
                zg_copy(block, d, matrix).wait_send()

    tile_row = lax.broadcasted_iota(jnp.int32, (HD, HD), 0)
    tile_col = lax.broadcasted_iota(jnp.int32, (HD, HD), 1)

    def softmax_part(scores, values):
        peak = jnp.max(scores, axis=1, keepdims=True)
        lifted = jnp.exp2((scores - peak) * SCALE)
        weight = jnp.sum(lifted, axis=1, keepdims=True)
        return mm(lifted.astype(BF16), values), peak * SCALE, weight

    def masked(scores, keep, last):
        width = scores.shape[1]
        if width == HD:
            return jnp.where(keep, scores, -1e30)
        if last:
            return jnp.concatenate([scores[:, : width - HD], jnp.where(keep, scores[:, width - HD :], -1e30)], axis=1)
        return jnp.concatenate([jnp.where(keep, scores[:, :HD], -1e30), scores[:, HD:]], axis=1)

    def far_tile(block, head, tile):
        lanes = pl.ds(head * HD, HD)
        q_copy(block, head, tile).wait_recv()
        source = jnp.maximum(block - place.last, 0)
        rows = pl.ds(tile * HD, HD)
        span = pl.ds(tile * HD, TOK - tile * HD)
        scores = mm_nt(q_land[block, rows, lanes], proj[1, source, span, lanes])
        scores = masked(scores, tile_col > tile_row, False)
        result, peak, weight = softmax_part(scores, proj[2, source, span, lanes])
        o_out[block, rows, lanes] = (result / weight).astype(BF16)
        log_sum = jnp.broadcast_to(peak + jnp.log2(weight), (HD, LANES)).T
        stat_out[block, head : head + 1, rows] = log_sum[:1]
        o_copy(block, head, tile).start()
        if head == HEADS - 1 and tile == 3:
            stat_copy(block).start()

    def near_item(block, head):
        lanes = pl.ds(head * HD, HD)
        for tile in range(4):
            o_copy(block, head, tile).wait_recv()
        if head == 0:
            stat_copy(block).wait_recv()
        for tile in range(4):
            rows = pl.ds(tile * HD, HD)
            span = pl.ds(0, (tile + 1) * HD)
            scores = mm_nt(proj[0, block, rows, lanes], proj[1, block, span, lanes])
            scores = masked(scores, tile_col <= tile_row, True)
            result, peak, weight = softmax_part(scores, proj[2, block, span, lanes])
            far_log = jnp.broadcast_to(stat_land[block, head : head + 1, rows], (LANES, HD)).T
            if block == 0:
                far_log = jnp.where(place.first, -1e30, far_log)
            top = jnp.maximum(peak, far_log)
            near_w = jnp.exp2(peak - top)
            far_w = jnp.exp2(far_log - top)
            far = o_land[block, rows, lanes].astype(F32)
            merged = (result * near_w + far * far_w) / (weight * near_w + far_w)
            attended[block, rows, lanes] = merged.astype(BF16)

    def query_part(block, weights, factors, part):
        rows = pl.ds(part * 256, 256)
        query = proj[0, block, rows, :]
        gate = mm(query, weights[0])
        up = mm(query, weights[1])
        if factors is not None:
            gate = gate * factors[0]
            up = up * factors[1]
        hidden_q = (gate * jax.nn.sigmoid(gate) * up).astype(BF16)
        result = mm(hidden_q, weights[2])
        if factors is not None:
            result = result * factors[2]
        fast = result * lax.rsqrt(jnp.mean(result * result, axis=1, keepdims=True) + 1e-05)
        mixed[place.head, block, rows, :] = (attended[block, rows, :].astype(F32) + fast).astype(BF16)

    def share(block):
        head_copy(block, 0).start()
        head_copy(block, 1).start()

    def forward(block):
        head_copy(block, 1).wait_recv()
        head_copy(block, 2).start()

    def project(block, turn):
        owner = (place.head, place.across, place.sibling, place.diagonal)[turn]
        if turn == 2:
            head_copy(block, 0).wait_recv()
        if turn == 3:
            head_copy(block, 2).wait_recv()
        product = mm(mixed[owner, block], wout[pl.ds(pl.multiple_of(owner * FD, FD), FD), :])
        if turn == 0:
            out_acc[...] = hidden[block].astype(F32) + product
        elif turn < 3:
            out_acc[...] += product
        else:
            out_stage[block] = (out_acc[...] + product).astype(BF16)
            pltpu.make_async_copy(out_stage.at[block], out_hbm.at[block], store_sem.at[block]).start()

    def run(steps, fillers):
        fillers = list(fillers)
        for count, _ in enumerate(steps):
            while fillers and fillers[0][0] <= count:
                fillers.pop(0)[1]()
        for _, filler in fillers:
            filler()

    for load in loads[:5]:
        load.wait()
    key_pass(0, [state[0], state[1], state[2]], None)
    for load in loads[5:]:
        load.wait()
    fillers = [
        (0, lambda: far_tile(0, 0, 0)),
        (0, lambda: far_tile(0, 0, 1)),
        (0, lambda: far_tile(0, 0, 2)),
        (0, lambda: q_copy(0, 2, 0).start()),
        (1, lambda: far_tile(0, 0, 3)),
        (1, lambda: q_copy(0, 2, 1).start()),
        (2, lambda: far_tile(0, 1, 0)),
        (2, lambda: q_copy(0, 2, 2).start()),
        (3, lambda: far_tile(0, 1, 1)),
        (3, lambda: q_copy(0, 2, 3).start()),
        (4, lambda: far_tile(0, 1, 2)),
        (4, lambda: q_copy(0, 3, 0).start()),
        (5, lambda: far_tile(0, 1, 3)),
        (5, lambda: q_copy(0, 3, 1).start()),
        (6, lambda: far_tile(0, 2, 0)),
        (6, lambda: q_copy(0, 3, 2).start()),
        (7, lambda: far_tile(0, 2, 1)),
        (7, lambda: q_copy(0, 3, 3).start()),
        (8, lambda: far_tile(0, 2, 2)),
        (8, lambda: q_copy(1, 0, 0).start()),
        (9, lambda: far_tile(0, 2, 3)),
        (9, lambda: q_copy(1, 0, 1).start()),
        (10, lambda: far_tile(0, 3, 0)),
        (10, lambda: q_copy(1, 0, 2).start()),
        (11, lambda: far_tile(0, 3, 1)),
        (11, lambda: q_copy(1, 0, 3).start()),
        (12, lambda: far_tile(0, 3, 2)),
        (12, lambda: q_copy(1, 1, 0).start()),
        (13, lambda: far_tile(0, 3, 3)),
        (13, lambda: q_copy(1, 1, 1).start()),
        (14, lambda: far_tile(1, 0, 0)),
        (14, lambda: q_copy(1, 1, 2).start()),
        (15, lambda: far_tile(1, 0, 1)),
        (15, lambda: q_copy(1, 1, 3).start()),
        (16, lambda: far_tile(1, 0, 2)),
        (16, lambda: q_copy(1, 2, 0).start()),
        (17, lambda: far_tile(1, 0, 3)),
        (17, lambda: q_copy(1, 2, 1).start()),
        (18, lambda: far_tile(1, 1, 0)),
        (18, lambda: q_copy(1, 2, 2).start()),
        (19, lambda: far_tile(1, 1, 1)),
        (19, lambda: q_copy(1, 2, 3).start()),
        (20, lambda: far_tile(1, 1, 2)),
        (20, lambda: q_copy(1, 3, 0).start()),
        (21, lambda: far_tile(1, 1, 3)),
        (21, lambda: q_copy(1, 3, 1).start()),
        (22, lambda: far_tile(1, 2, 0)),
        (22, lambda: q_copy(1, 3, 2).start()),
        (23, lambda: far_tile(1, 2, 1)),
        (23, lambda: q_copy(1, 3, 3).start()),
        (24, lambda: far_tile(1, 2, 2)),
        (25, lambda: far_tile(1, 2, 3)),
        (26, lambda: far_tile(1, 3, 0)),
    ]
    run(reduction(0, None), fillers)

    norm = []
    factors = []
    for matrix in range(3):
        first = jnp.sqrt(square_sum(state[matrix].astype(F32)))
        second = square_sum(moved0[matrix].astype(F32))
        factors.append(first * lax.rsqrt(second + 1e-06))
        norm.append(jnp.sqrt(second) * factors[matrix])
    key_pass(1, [moved0[0], moved0[1], moved0[2]], factors)
    fillers = [
        (0, lambda: far_tile(1, 3, 1)),
        (1, lambda: far_tile(1, 3, 2)),
        (2, lambda: far_tile(1, 3, 3)),
        (4, lambda: near_item(0, 0)),
        (5, lambda: near_item(0, 1)),
        (6, lambda: near_item(0, 2)),
        (7, lambda: near_item(0, 3)),
        (8, lambda: query_part(0, [state[0], state[1], state[2]], None, 0)),
        (9, lambda: query_part(0, [state[0], state[1], state[2]], None, 1)),
        (9, lambda: share(0)),
        (9, lambda: near_item(1, 0)),
        (10, lambda: near_item(1, 1)),
        (11, lambda: near_item(1, 2)),
        (12, lambda: near_item(1, 3)),
        (13, lambda: query_part(1, [moved0[0], moved0[1], moved0[2]], factors, 0)),
        (14, lambda: query_part(1, [moved0[0], moved0[1], moved0[2]], factors, 1)),
        (14, lambda: share(1)),
        (15, lambda: forward(0)),
        (15, lambda: project(0, 0)),
        (16, lambda: project(0, 1)),
        (17, lambda: project(0, 2)),
        (18, lambda: project(0, 3)),
        (19, lambda: forward(1)),
        (19, lambda: project(1, 0)),
        (20, lambda: project(1, 1)),
        (21, lambda: project(1, 2)),
        (22, lambda: project(1, 3)),
    ]
    run(reduction(1, factors), fillers)

    finals = [
        pltpu.make_async_copy(moved1.at[0], up_out.at[0, 0], store_sem.at[2]),
        pltpu.make_async_copy(moved1.at[1], up_out.at[1, 0], store_sem.at[3]),
        pltpu.make_async_copy(moved1.at[2], down_out.at[0], store_sem.at[4]),
    ]
    for final in finals:
        final.start()
    for matrix in range(3):
        last = square_sum(moved1[matrix].astype(F32))
        factor = norm[matrix] * lax.rsqrt(last + 1e-06)
        factor_out[matrix] = jnp.broadcast_to(factor, (8, LANES))
    for block in range(BLOCKS):
        for head in range(HEADS):
            for tile in range(4):
                q_copy(block, head, tile).wait_send()
                o_copy(block, head, tile).wait_send()
        stat_copy(block).wait_send()
        for kind in range(3):
            head_copy(block, kind).wait_send()
        pltpu.make_async_copy(out_stage.at[block], out_hbm.at[block], store_sem.at[block]).wait()
    for final in finals:
        final.wait()


def body(hidden_in, projected, w_out, fast_up, fast_down, learn_rates):
    dma = pltpu.SemaphoreType.DMA
    vmem = pltpu.VMEM
    hbm_spec = pl.BlockSpec(memory_space=pl.ANY)
    vmem_spec = pl.BlockSpec(memory_space=pltpu.VMEM)
    square = (FD, FD)
    layer_out, up_moved, down_moved, factor = pl.pallas_call(
        layer_kernel,
        out_shape=(
            jax.ShapeDtypeStruct((BLOCKS, TOK, FD), BF16),
            jax.ShapeDtypeStruct((2, 1, FD, FD), BF16),
            jax.ShapeDtypeStruct((1, FD, FD), BF16),
            jax.ShapeDtypeStruct((3, 8, LANES), F32),
        ),
        in_specs=[hbm_spec] * 5 + [vmem_spec],
        out_specs=(hbm_spec, hbm_spec, hbm_spec, vmem_spec),
        scratch_shapes=[
            vmem((3, BLOCKS, TOK, FD), BF16),
            vmem((BLOCKS, TOK, FD), BF16),
            vmem((4 * FD, FD), BF16),
            vmem((3,) + square, BF16),
            vmem((BLOCKS, TOK, FD), BF16),
            vmem((BLOCKS, TOK, FD), BF16),
            vmem((BLOCKS, TOK, FD), BF16),
            vmem((BLOCKS, 8, TOK), F32),
            vmem((BLOCKS, 8, TOK), F32),
            vmem((BLOCKS, TOK, FD), BF16),
            vmem((4, BLOCKS, TOK, FD), BF16),
            vmem((3,) + square, BF16),
            vmem((3,) + square, F32),
            vmem((3,) + square, BF16),
            vmem((3,) + square, BF16),
            vmem((3, COLOURS, 256, LANES), BF16),
            vmem((3, COLOURS, 128, LANES), BF16),
            vmem((3, COLOURS, 64, LANES), BF16),
            vmem((3, COLOURS, 32, LANES), BF16),
            vmem((3, 3, 32, LANES), BF16),
            vmem((3, 32, LANES), F32),
            vmem(square, BF16),
            vmem(square, BF16),
            vmem(square, BF16),
            vmem(square, BF16),
            vmem((BLOCKS, TOK, FD), BF16),
            vmem(square, F32),
            dma((10,)),
            dma((5,)),
            dma((32,)),
            dma((32,)),
            dma((32,)),
            dma((32,)),
            dma((2,)),
            dma((2,)),
            dma((2, 3)),
            dma((2, 3)),
            dma((4, 3, COLOURS)),
            dma((4, 3, COLOURS)),
            dma((3, 3)),
            dma((3, 3)),
            dma((4, 3, COLOURS)),
            dma((4, 3, COLOURS)),
            dma((3, 3)),
            dma((3, 3)),
        ],
        compiler_params=pltpu.CompilerParams(
            collective_id=0, has_side_effects=True, vmem_limit_bytes=60 << 20
        ),
    )(hidden_in, projected, w_out, fast_up, fast_down, learn_rates)
    return (
        layer_out,
        up_moved.astype(F32) * factor[:2, None, :1, :1],
        down_moved.astype(F32) * factor[2:, :1, :1],
    )


def solution(mesh):
    in_specs = (
        P(None, "ctx", "head"),
        P(None, None, "ctx", "head"),
        P(None, "head"),
        P(None, "head", None, None),
        P("head", None, None),
        P("head", None, "ctx"),
    )
    out_specs = (P(None, "ctx", "head"), P(None, "head", None, None), P("head", None, None))
    return jax.shard_map(body, mesh=mesh, in_specs=in_specs, out_specs=out_specs, check_vma=False)
```

```python
import math

import jax
import jax.numpy as jnp
from jax import lax
from jax.experimental import pallas as pl
from jax.experimental.pallas import tpu as pltpu
from jax.sharding import PartitionSpec as P

MESH = pl.DeviceIdType.MESH
F32 = jnp.float32
BF16 = jnp.bfloat16
HD = 128
FD = 512
TOK = 512
HEADS = 4
BLOCKS = 2
BLOCK_LEN = 32768
LANES = 128
COLOURS = 4
SCALE = math.log2(math.e) / math.sqrt(HD)
ORDER = (
    ("x1", "x3", "y1", "y3"),
    ("x3", "x1", "y3", "y1"),
    ("y1", "y3", "x1", "x3"),
    ("y3", "y1", "x3", "x1"),
)


class Place:
    def __init__(self):
        ctx = lax.axis_index("ctx")
        self.head = lax.axis_index("head")
        self.x = ctx // 16
        self.z = (ctx // 4) % 4
        self.y = ctx % 4
        x_low, x_high = self.x % 2, self.x // 2
        y_low, y_high = self.y % 2, self.y // 2
        self.key = {
            "x1": (x_low + x_high) % 2,
            "x3": x_high,
            "y1": (y_low + y_high) % 2,
            "y3": y_high,
        }
        self.partner = {
            "x1": self.at(self.x + 1 - 2 * x_low, self.z, self.y),
            "x3": self.at(3 - self.x, self.z, self.y),
            "y1": self.at(self.x, self.z, self.y + 1 - 2 * y_low),
            "y3": self.at(self.x, self.z, 3 - self.y),
        }
        self.along_x = [self.at((self.x + d) % 4, self.z, self.y) for d in (1, 2, 3)]
        self.along_y = [self.at(self.x, self.z, (self.y + d) % 4) for d in (1, 2, 3)]
        self.z_peer = [self.at(self.x, (self.z + d) % 4, self.y) for d in (1, 2, 3)]
        self.z_to = [(self.z + d) % 4 for d in (1, 2, 3)]
        self.before = ((ctx + 63) % 64, self.head)
        self.after = ((ctx + 1) % 64, self.head)
        self.sibling = self.head + 1 - 2 * (self.head % 2)
        self.across = (self.head + 2) % 4
        self.diagonal = (self.sibling + 2) % 4
        self.to_sibling = (ctx, self.sibling)
        self.to_across = (ctx, self.across)
        self.first = ctx == 0
        self.last = ctx // 63
        self.keep, self.send, self.mine = [], [], []
        self.fan_rows, self.fan_peers = [], []
        for colour in range(COLOURS):
            keeps, sends, off = [], [], 0
            for step in range(2):
                length = 256 >> step
                key = self.key[ORDER[colour][step]]
                keeps.append(pl.multiple_of(off + key * length, 32))
                sends.append(pl.multiple_of(off + (1 - key) * length, 32))
                off = off + key * length
            self.keep.append(keeps)
            self.send.append(sends)
            turn = self.y if colour < 2 else self.x
            self.mine.append(pl.multiple_of(off + turn * 32, 32))
            self.fan_rows.append([pl.multiple_of(off + (turn + d) % 4 * 32, 32) for d in (1, 2, 3)])
            self.fan_peers.append(self.along_y if colour < 2 else self.along_x)

    def at(self, x, z, y):
        return (x * 16 + z * 4 + y, self.head)

    def rows_of(self, colour):
        row = 0
        for which in range(COLOURS):
            row = row + jnp.where(colour == which, self.mine[which], 0)
        return pl.multiple_of(row, 32)


def remote(src, dst, send_sem, recv_sem, other):
    return pltpu.make_async_remote_copy(
        src_ref=src, dst_ref=dst, send_sem=send_sem, recv_sem=recv_sem, device_id=other, device_id_type=MESH
    )


def block_of(ref, matrix, row, length, colour):
    if isinstance(colour, int):
        lanes = pl.ds(colour * LANES, LANES)
    else:
        lanes = pl.ds(pl.multiple_of(colour * LANES, LANES), LANES)
    return ref.at[matrix, pl.ds(row, length), lanes]


def mm(a, b):
    return lax.dot_general(a, b, (((1,), (0,)), ((), ())), preferred_element_type=F32)


def mm_nt(a, b):
    return lax.dot_general(a, b, (((1,), (1,)), ((), ())), preferred_element_type=F32)


def mm_tn(a, b):
    return lax.dot_general(a, b, (((0,), (0,)), ((), ())), preferred_element_type=F32)


def square_sum(value):
    rows = jnp.sum(value * value, axis=0, keepdims=True)
    return jnp.sum(rows, axis=1, keepdims=True)


def layer_kernel(
    hidden_hbm, proj_hbm, wout_hbm, up_hbm, down_hbm, rates,
    out_hbm, up_out, down_out, factor_out,
    proj, hidden, wout, state, q_land, o_out, o_land, stat_out, stat_land, attended, mixed, grad, total, moved0, moved1,
    land0, land1, fan_land, z_land, piece, hid, gate_g, up_g, out_g, out_stage, out_acc,
    load_sem, store_sem, q_send, q_recv, o_send, o_recv, st_send, st_recv, h_send, h_recv,
    s_send, s_recv, z_send, z_recv, g_send, g_recv, zg_send, zg_recv, fan_send, fan_recv, fg_send, fg_recv,
):
    place = Place()
    lands = (land0, land1)
    moved = (moved0, moved1)

    loads = [
        pltpu.make_async_copy(proj_hbm.at[1, 0], proj.at[1, 0], load_sem.at[0]),
        pltpu.make_async_copy(proj_hbm.at[2, 0], proj.at[2, 0], load_sem.at[1]),
        pltpu.make_async_copy(up_hbm.at[0, 0], state.at[0], load_sem.at[2]),
        pltpu.make_async_copy(up_hbm.at[1, 0], state.at[1], load_sem.at[3]),
        pltpu.make_async_copy(down_hbm.at[0], state.at[2], load_sem.at[4]),
        pltpu.make_async_copy(proj_hbm.at[0], proj.at[0], load_sem.at[5]),
        pltpu.make_async_copy(proj_hbm.at[1, 1], proj.at[1, 1], load_sem.at[6]),
        pltpu.make_async_copy(proj_hbm.at[2, 1], proj.at[2, 1], load_sem.at[7]),
        pltpu.make_async_copy(wout_hbm, wout, load_sem.at[8]),
        pltpu.make_async_copy(hidden_hbm, hidden, load_sem.at[9]),
    ]
    for load in loads:
        load.start()

    barrier = pltpu.get_barrier_semaphore()
    others = place.along_x + place.along_y + place.z_peer
    others += [place.before, place.after, place.to_sibling, place.to_across]
    for other in others:
        pl.semaphore_signal(barrier, inc=1, device_id=other, device_id_type=MESH)
    pl.semaphore_wait(barrier, len(others))

    def q_copy(block, head, tile):
        lanes, rows = pl.ds(head * HD, HD), pl.ds(tile * HD, HD)
        sem = (block * HEADS + head) * 4 + tile
        return remote(
            proj_hbm.at[0, block, rows, lanes], q_land.at[block, rows, lanes], q_send.at[sem], q_recv.at[sem], place.before
        )

    def o_copy(block, head, tile):
        lanes, rows = pl.ds(head * HD, HD), pl.ds(tile * HD, HD)
        sem = (block * HEADS + head) * 4 + tile
        return remote(
            o_out.at[block, rows, lanes], o_land.at[block, rows, lanes], o_send.at[sem], o_recv.at[sem], place.after
        )

    def stat_copy(block):
        return remote(stat_out.at[block], stat_land.at[block], st_send.at[block], st_recv.at[block], place.after)

    def head_copy(block, kind):
        owner, to = (
            (place.head, place.to_sibling),
            (place.head, place.to_across),
            (place.across, place.to_sibling),
        )[kind]
        rows = mixed.at[owner, block]
        return remote(rows, rows, h_send.at[block, kind], h_recv.at[block, kind], to)

    def scatter_copy(step, matrix, colour):
        length = 256 >> step
        return remote(
            block_of(grad, matrix, place.send[colour][step], length, colour),
            lands[step].at[matrix, colour],
            s_send.at[step, matrix, colour],
            s_recv.at[step, matrix, colour],
            place.partner[ORDER[colour][step]],
        )

    def fan_copy(matrix, colour, d):
        return remote(
            block_of(grad, matrix, place.fan_rows[colour][d], 32, colour),
            fan_land.at[d, matrix, colour],
            fan_send.at[d, matrix, colour],
            fan_recv.at[d, matrix, colour],
            place.fan_peers[colour][d],
        )

    def fan_gather(block, matrix, colour, d):
        own = block_of(moved[block], matrix, place.mine[colour], 32, colour)
        return remote(
            own, own, fg_send.at[d, matrix, colour], fg_recv.at[d, matrix, colour], place.fan_peers[colour][d]
        )

    def z_copy(d, matrix):
        to = place.z_to[d]
        return remote(
            block_of(grad, matrix, place.rows_of(to), 32, to),
            z_land.at[d, matrix],
            z_send.at[d, matrix],
            z_recv.at[d, matrix],
            place.z_peer[d],
        )

    own_row = place.rows_of(place.z)

    def zg_copy(block, d, matrix):
        own = block_of(moved[block], matrix, own_row, 32, place.z)
        return remote(own, own, zg_send.at[d, matrix], zg_recv.at[d, matrix], place.z_peer[d])

    def gather_copy(block, step, matrix, colour):
        kept = block_of(moved[block], matrix, place.keep[colour][step], 256 >> step, colour)
        return remote(
            kept,
            kept,
            g_send.at[step, matrix, colour],
            g_recv.at[step, matrix, colour],
            place.partner[ORDER[colour][step]],
        )

    q_copy(0, 0, 0).start()
    q_copy(0, 0, 1).start()
    q_copy(0, 0, 2).start()
    q_copy(0, 0, 3).start()
    q_copy(0, 1, 0).start()
    q_copy(0, 1, 1).start()
    q_copy(0, 1, 2).start()
    q_copy(0, 1, 3).start()

    def key_pass(block, weights, factors):
        step_scale = -1.0 / math.sqrt(BLOCK_LEN)

        def grown(value, which):
            return value if factors is None else value * factors[which]

        rows_per = 256
        for part in range(TOK // rows_per):
            rows = pl.ds(part * rows_per, rows_per)
            key = proj[1, block, rows, :]
            rate = rates[0, block : block + 1, part * rows_per : (part + 1) * rows_per] * step_scale
            rate = jnp.broadcast_to(rate, (LANES, rows_per)).T
            value = proj[2, block, rows, :].astype(F32)
            out_grad = (value * jnp.concatenate([rate] * 4, axis=1)).astype(BF16)
            out_g[rows, :] = out_grad
            gate = grown(mm(key, weights[0]), 0)
            up = grown(mm(key, weights[1]), 1)
            back = grown(mm_nt(out_grad, weights[2]), 2)
            sig = jax.nn.sigmoid(gate)
            gate_sig = gate * sig
            hid[rows, :] = (gate_sig * up).astype(BF16)
            gate_g[rows, :] = (back * up * (sig + gate_sig * (1.0 - sig))).astype(BF16)
            up_g[rows, :] = (back * gate_sig).astype(BF16)
        for matrix in (2, 1, 0):
            if matrix == 2:
                sums = mm_tn(hid[...], out_g[...])
            elif matrix == 1:
                sums = mm_tn(proj[1, block], up_g[...])
            else:
                sums = mm_tn(proj[1, block], gate_g[...])
            total[matrix] = sums
            grad[matrix] = sums.astype(BF16)
            for colour in range(COLOURS):
                scatter_copy(0, matrix, colour).start()

    def reduction(block, old_factors):
        for step in range(2):
            length = 256 >> step
            for matrix in (2, 1, 0):
                for colour in range(COLOURS):
                    scatter_copy(step, matrix, colour).wait_recv()
                    row = place.keep[colour][step]
                    kept = block_of(total, matrix, row, length, colour)
                    value = kept[...] + lands[step][matrix, colour].astype(F32)
                    kept[...] = value
                    block_of(grad, matrix, row, length, colour)[...] = value.astype(BF16)
                    if step == 0:
                        scatter_copy(1, matrix, colour).start()
                    else:
                        for d in (1, 0, 2):
                            fan_copy(matrix, colour, d).start()
                yield
        for matrix in (2, 1, 0):
            for colour in range(COLOURS):
                kept = block_of(total, matrix, place.mine[colour], 32, colour)
                value = kept[...]
                for d in range(3):
                    fan_copy(matrix, colour, d).wait_recv()
                    value = value + fan_land[d, matrix, colour].astype(F32)
                kept[...] = value
                block_of(grad, matrix, place.mine[colour], 32, colour)[...] = value.astype(BF16)
            for d in range(3):
                z_copy(d, matrix).start()
            yield
        for matrix in (2, 1, 0):
            value = block_of(total, matrix, own_row, 32, place.z)[...]
            for d in range(3):
                z_copy(d, matrix).wait_recv()
                value = value + z_land[d, matrix].astype(F32)
            if block == 0:
                value = block_of(state, matrix, own_row, 32, place.z)[...].astype(F32) - value
                piece[matrix] = value
            else:
                value = piece[matrix] * old_factors[matrix] - value
            block_of(moved[block], matrix, own_row, 32, place.z)[...] = value.astype(BF16)
            for d in range(3):
                zg_copy(block, d, matrix).start()
            yield
        for matrix in (2, 1, 0):
            for d in range(3):
                zg_copy(block, d, matrix).wait_recv()
            for d in (1, 0, 2):
                for colour in range(COLOURS):
                    fan_gather(block, matrix, colour, d).start()
            yield
        for step in (1, 0):
            for matrix in (2, 1, 0):
                for colour in range(COLOURS):
                    if step == 1:
                        for d in range(3):
                            fan_gather(block, matrix, colour, d).wait_recv()
                    else:
                        gather_copy(block, 1, matrix, colour).wait_recv()
                    gather_copy(block, step, matrix, colour).start()
                yield
        for matrix in (2, 1, 0):
            for colour in range(COLOURS):
                gather_copy(block, 0, matrix, colour).wait_recv()
        for matrix in range(3):
            for colour in range(COLOURS):
                for step in range(2):
                    scatter_copy(step, matrix, colour).wait_send()
                    gather_copy(block, step, matrix, colour).wait_send()
                for d in range(3):
                    fan_copy(matrix, colour, d).wait_send()
                    fan_gather(block, matrix, colour, d).wait_send()
            for d in range(3):
                z_copy(d, matrix).wait_send()
                zg_copy(block, d, matrix).wait_send()

    tile_row = lax.broadcasted_iota(jnp.int32, (HD, HD), 0)
    tile_col = lax.broadcasted_iota(jnp.int32, (HD, HD), 1)

    def softmax_part(scores, values):
        peak = jnp.max(scores, axis=1, keepdims=True)
        lifted = jnp.exp2((scores - peak) * SCALE)
        weight = jnp.sum(lifted, axis=1, keepdims=True)
        return mm(lifted.astype(BF16), values), peak * SCALE, weight

    def masked(scores, keep, last):
        width = scores.shape[1]
        if width == HD:
            return jnp.where(keep, scores, -1e30)
        if last:
            return jnp.concatenate([scores[:, : width - HD], jnp.where(keep, scores[:, width - HD :], -1e30)], axis=1)
        return jnp.concatenate([jnp.where(keep, scores[:, :HD], -1e30), scores[:, HD:]], axis=1)

    def far_tile(block, head, tile):
        lanes = pl.ds(head * HD, HD)
        q_copy(block, head, tile).wait_recv()
        source = jnp.maximum(block - place.last, 0)
        rows = pl.ds(tile * HD, HD)
        span = pl.ds(tile * HD, TOK - tile * HD)
        scores = mm_nt(q_land[block, rows, lanes], proj[1, source, span, lanes])
        scores = masked(scores, tile_col > tile_row, False)
        result, peak, weight = softmax_part(scores, proj[2, source, span, lanes])
        o_out[block, rows, lanes] = (result / weight).astype(BF16)
        log_sum = jnp.broadcast_to(peak + jnp.log2(weight), (HD, LANES)).T
        stat_out[block, head : head + 1, rows] = log_sum[:1]
        o_copy(block, head, tile).start()
        if head == HEADS - 1 and tile == 3:
            stat_copy(block).start()

    def near_item(block, head):
        lanes = pl.ds(head * HD, HD)
        for tile in range(4):
            o_copy(block, head, tile).wait_recv()
        if head == 0:
            stat_copy(block).wait_recv()
        for tile in range(4):
            rows = pl.ds(tile * HD, HD)
            span = pl.ds(0, (tile + 1) * HD)
            scores = mm_nt(proj[0, block, rows, lanes], proj[1, block, span, lanes])
            scores = masked(scores, tile_col <= tile_row, True)
            result, peak, weight = softmax_part(scores, proj[2, block, span, lanes])
            far_log = jnp.broadcast_to(stat_land[block, head : head + 1, rows], (LANES, HD)).T
            if block == 0:
                far_log = jnp.where(place.first, -1e30, far_log)
            top = jnp.maximum(peak, far_log)
            near_w = jnp.exp2(peak - top)
            far_w = jnp.exp2(far_log - top)
            far = o_land[block, rows, lanes].astype(F32)
            merged = (result * near_w + far * far_w) / (weight * near_w + far_w)
            attended[block, rows, lanes] = merged.astype(BF16)

    def query_part(block, weights, factors, part):
        rows = pl.ds(part * 256, 256)
        query = proj[0, block, rows, :]
        gate = mm(query, weights[0])
        up = mm(query, weights[1])
        if factors is not None:
            gate = gate * factors[0]
            up = up * factors[1]
        hidden_q = (gate * jax.nn.sigmoid(gate) * up).astype(BF16)
        result = mm(hidden_q, weights[2])
        if factors is not None:
            result = result * factors[2]
        fast = result * lax.rsqrt(jnp.mean(result * result, axis=1, keepdims=True) + 1e-05)
        mixed[place.head, block, rows, :] = (attended[block, rows, :].astype(F32) + fast).astype(BF16)

    def share(block):
        head_copy(block, 0).start()
        head_copy(block, 1).start()

    def forward(block):
        head_copy(block, 1).wait_recv()
        head_copy(block, 2).start()

    def project(block, turn):
        owner = (place.head, place.across, place.sibling, place.diagonal)[turn]
        if turn == 2:
            head_copy(block, 0).wait_recv()
        if turn == 3:
            head_copy(block, 2).wait_recv()
        product = mm(mixed[owner, block], wout[pl.ds(pl.multiple_of(owner * FD, FD), FD), :])
        if turn == 0:
            out_acc[...] = hidden[block].astype(F32) + product
        elif turn < 3:
            out_acc[...] += product
        else:
            out_stage[block] = (out_acc[...] + product).astype(BF16)
            pltpu.make_async_copy(out_stage.at[block], out_hbm.at[block], store_sem.at[block]).start()

    def run(steps, fillers):
        fillers = list(fillers)
        for count, _ in enumerate(steps):
            while fillers and fillers[0][0] <= count:
                fillers.pop(0)[1]()
        for _, filler in fillers:
            filler()

    for load in loads[:5]:
        load.wait()
    key_pass(0, [state[0], state[1], state[2]], None)
    for load in loads[5:]:
        load.wait()
    fillers = [
        (0, lambda: far_tile(0, 0, 0)),
        (0, lambda: far_tile(0, 0, 1)),
        (0, lambda: far_tile(0, 0, 2)),
        (0, lambda: far_tile(0, 0, 3)),
        (0, lambda: q_copy(0, 2, 0).start()),
        (1, lambda: far_tile(0, 1, 0)),
        (1, lambda: q_copy(0, 2, 1).start()),
        (2, lambda: far_tile(0, 1, 1)),
        (2, lambda: q_copy(0, 2, 2).start()),
        (3, lambda: far_tile(0, 1, 2)),
        (3, lambda: q_copy(0, 2, 3).start()),
        (4, lambda: far_tile(0, 1, 3)),
        (4, lambda: q_copy(0, 3, 0).start()),
        (5, lambda: far_tile(0, 2, 0)),
        (5, lambda: q_copy(0, 3, 1).start()),
        (6, lambda: far_tile(0, 2, 1)),
        (6, lambda: q_copy(0, 3, 2).start()),
        (7, lambda: far_tile(0, 2, 2)),
        (7, lambda: q_copy(0, 3, 3).start()),
        (8, lambda: far_tile(0, 2, 3)),
        (8, lambda: q_copy(1, 0, 0).start()),
        (9, lambda: far_tile(0, 3, 0)),
        (9, lambda: q_copy(1, 0, 1).start()),
        (10, lambda: far_tile(0, 3, 1)),
        (10, lambda: q_copy(1, 0, 2).start()),
        (11, lambda: far_tile(0, 3, 2)),
        (11, lambda: q_copy(1, 0, 3).start()),
        (12, lambda: far_tile(0, 3, 3)),
        (12, lambda: q_copy(1, 1, 0).start()),
        (13, lambda: far_tile(1, 0, 0)),
        (13, lambda: q_copy(1, 1, 1).start()),
        (14, lambda: far_tile(1, 0, 1)),
        (14, lambda: q_copy(1, 1, 2).start()),
        (15, lambda: far_tile(1, 0, 2)),
        (15, lambda: q_copy(1, 1, 3).start()),
        (16, lambda: far_tile(1, 0, 3)),
        (16, lambda: q_copy(1, 2, 0).start()),
        (17, lambda: far_tile(1, 1, 0)),
        (17, lambda: q_copy(1, 2, 1).start()),
        (18, lambda: far_tile(1, 1, 1)),
        (18, lambda: q_copy(1, 2, 2).start()),
        (19, lambda: far_tile(1, 1, 2)),
        (19, lambda: q_copy(1, 2, 3).start()),
        (20, lambda: far_tile(1, 1, 3)),
        (20, lambda: q_copy(1, 3, 0).start()),
    ]
    run(reduction(0, None), fillers)

    norm = []
    factors = []
    for matrix in range(3):
        first = jnp.sqrt(square_sum(state[matrix].astype(F32)))
        second = square_sum(moved0[matrix].astype(F32))
        factors.append(first * lax.rsqrt(second + 1e-06))
        norm.append(jnp.sqrt(second) * factors[matrix])
    key_pass(1, [moved0[0], moved0[1], moved0[2]], factors)
    fillers = [
        (0, lambda: far_tile(1, 2, 0)),
        (0, lambda: q_copy(1, 3, 1).start()),
        (1, lambda: far_tile(1, 2, 1)),
        (1, lambda: q_copy(1, 3, 2).start()),
        (2, lambda: far_tile(1, 2, 2)),
        (2, lambda: q_copy(1, 3, 3).start()),
        (3, lambda: far_tile(1, 2, 3)),
        (4, lambda: far_tile(1, 3, 0)),
        (5, lambda: far_tile(1, 3, 1)),
        (5, lambda: near_item(0, 0)),
        (5, lambda: near_item(0, 1)),
        (6, lambda: far_tile(1, 3, 2)),
        (6, lambda: near_item(0, 2)),
        (6, lambda: near_item(0, 3)),
        (7, lambda: far_tile(1, 3, 3)),
        (7, lambda: query_part(0, [state[0], state[1], state[2]], None, 0)),
        (8, lambda: query_part(0, [state[0], state[1], state[2]], None, 1)),
        (8, lambda: share(0)),
        (9, lambda: near_item(1, 0)),
        (9, lambda: near_item(1, 1)),
        (10, lambda: near_item(1, 2)),
        (10, lambda: near_item(1, 3)),
        (11, lambda: query_part(1, [moved0[0], moved0[1], moved0[2]], factors, 0)),
        (12, lambda: query_part(1, [moved0[0], moved0[1], moved0[2]], factors, 1)),
        (12, lambda: share(1)),
        (12, lambda: forward(0)),
        (12, lambda: project(0, 0)),
        (13, lambda: project(0, 1)),
        (13, lambda: project(0, 2)),
        (14, lambda: project(0, 3)),
        (15, lambda: forward(1)),
        (15, lambda: project(1, 0)),
        (15, lambda: project(1, 1)),
        (16, lambda: project(1, 2)),
        (16, lambda: project(1, 3)),
    ]
    run(reduction(1, factors), fillers)

    finals = [
        pltpu.make_async_copy(moved1.at[0], up_out.at[0, 0], store_sem.at[2]),
        pltpu.make_async_copy(moved1.at[1], up_out.at[1, 0], store_sem.at[3]),
        pltpu.make_async_copy(moved1.at[2], down_out.at[0], store_sem.at[4]),
    ]
    for final in finals:
        final.start()
    for matrix in range(3):
        last = square_sum(moved1[matrix].astype(F32))
        factor = norm[matrix] * lax.rsqrt(last + 1e-06)
        factor_out[matrix] = jnp.broadcast_to(factor, (8, LANES))
    for block in range(BLOCKS):
        for head in range(HEADS):
            for tile in range(4):
                q_copy(block, head, tile).wait_send()
                o_copy(block, head, tile).wait_send()
        stat_copy(block).wait_send()
        for kind in range(3):
            head_copy(block, kind).wait_send()
        pltpu.make_async_copy(out_stage.at[block], out_hbm.at[block], store_sem.at[block]).wait()
    for final in finals:
        final.wait()


def body(hidden_in, projected, w_out, fast_up, fast_down, learn_rates):
    dma = pltpu.SemaphoreType.DMA
    vmem = pltpu.VMEM
    hbm_spec = pl.BlockSpec(memory_space=pl.ANY)
    vmem_spec = pl.BlockSpec(memory_space=pltpu.VMEM)
    square = (FD, FD)
    layer_out, up_moved, down_moved, factor = pl.pallas_call(
        layer_kernel,
        out_shape=(
            jax.ShapeDtypeStruct((BLOCKS, TOK, FD), BF16),
            jax.ShapeDtypeStruct((2, 1, FD, FD), BF16),
            jax.ShapeDtypeStruct((1, FD, FD), BF16),
            jax.ShapeDtypeStruct((3, 8, LANES), F32),
        ),
        in_specs=[hbm_spec] * 5 + [vmem_spec],
        out_specs=(hbm_spec, hbm_spec, hbm_spec, vmem_spec),
        scratch_shapes=[
            vmem((3, BLOCKS, TOK, FD), BF16),
            vmem((BLOCKS, TOK, FD), BF16),
            vmem((4 * FD, FD), BF16),
            vmem((3,) + square, BF16),
            vmem((BLOCKS, TOK, FD), BF16),
            vmem((BLOCKS, TOK, FD), BF16),
            vmem((BLOCKS, TOK, FD), BF16),
            vmem((BLOCKS, 8, TOK), F32),
            vmem((BLOCKS, 8, TOK), F32),
            vmem((BLOCKS, TOK, FD), BF16),
            vmem((4, BLOCKS, TOK, FD), BF16),
            vmem((3,) + square, BF16),
            vmem((3,) + square, F32),
            vmem((3,) + square, BF16),
            vmem((3,) + square, BF16),
            vmem((3, COLOURS, 256, LANES), BF16),
            vmem((3, COLOURS, 128, LANES), BF16),
            vmem((3, 3, COLOURS, 32, LANES), BF16),
            vmem((3, 3, 32, LANES), BF16),
            vmem((3, 32, LANES), F32),
            vmem(square, BF16),
            vmem(square, BF16),
            vmem(square, BF16),
            vmem(square, BF16),
            vmem((BLOCKS, TOK, FD), BF16),
            vmem(square, F32),
            dma((10,)),
            dma((5,)),
            dma((32,)),
            dma((32,)),
            dma((32,)),
            dma((32,)),
            dma((2,)),
            dma((2,)),
            dma((2, 3)),
            dma((2, 3)),
            dma((2, 3, COLOURS)),
            dma((2, 3, COLOURS)),
            dma((3, 3)),
            dma((3, 3)),
            dma((2, 3, COLOURS)),
            dma((2, 3, COLOURS)),
            dma((3, 3)),
            dma((3, 3)),
            dma((3, 3, COLOURS)),
            dma((3, 3, COLOURS)),
            dma((3, 3, COLOURS)),
            dma((3, 3, COLOURS)),
        ],
        compiler_params=pltpu.CompilerParams(
            collective_id=0, has_side_effects=True, vmem_limit_bytes=60 << 20
        ),
    )(hidden_in, projected, w_out, fast_up, fast_down, learn_rates)
    return (
        layer_out,
        up_moved.astype(F32) * factor[:2, None, :1, :1],
        down_moved.astype(F32) * factor[2:, :1, :1],
    )


def solution(mesh):
    in_specs = (
        P(None, "ctx", "head"),
        P(None, None, "ctx", "head"),
        P(None, "head"),
        P(None, "head", None, None),
        P("head", None, None),
        P("head", None, "ctx"),
    )
    out_specs = (P(None, "ctx", "head"), P(None, "head", None, None), P("head", None, None))
    return jax.shard_map(body, mesh=mesh, in_specs=in_specs, out_specs=out_specs, check_vma=False)
```

```python
import math

import jax
import jax.numpy as jnp
from jax import lax
from jax.experimental import pallas as pl
from jax.experimental.pallas import tpu as pltpu
from jax.sharding import PartitionSpec as P

MESH = pl.DeviceIdType.MESH
F32 = jnp.float32
BF16 = jnp.bfloat16
HD = 128
FD = 512
TOK = 512
HEADS = 4
BLOCKS = 2
BLOCK_LEN = 32768
LANES = 128
COLOURS = 4
SCALE = math.log2(math.e) / math.sqrt(HD)
ORDER = (
    ("x1", "x3", "y1", "y3"),
    ("x3", "x1", "y3", "y1"),
    ("y1", "y3", "x1", "x3"),
    ("y3", "y1", "x3", "x1"),
)


class Place:
    def __init__(self):
        ctx = lax.axis_index("ctx")
        self.head = lax.axis_index("head")
        self.x = ctx // 16
        self.z = (ctx // 4) % 4
        self.y = ctx % 4
        x_low, x_high = self.x % 2, self.x // 2
        y_low, y_high = self.y % 2, self.y // 2
        self.key = {
            "x1": (x_low + x_high) % 2,
            "x3": x_high,
            "y1": (y_low + y_high) % 2,
            "y3": y_high,
        }
        self.partner = {
            "x1": self.at(self.x + 1 - 2 * x_low, self.z, self.y),
            "x3": self.at(3 - self.x, self.z, self.y),
            "y1": self.at(self.x, self.z, self.y + 1 - 2 * y_low),
            "y3": self.at(self.x, self.z, 3 - self.y),
        }
        self.along_x = [self.at((self.x + d) % 4, self.z, self.y) for d in (1, 2, 3)]
        self.along_y = [self.at(self.x, self.z, (self.y + d) % 4) for d in (1, 2, 3)]
        self.z_peer = [self.at(self.x, (self.z + d) % 4, self.y) for d in (1, 2, 3)]
        self.z_to = [(self.z + d) % 4 for d in (1, 2, 3)]
        self.before = ((ctx + 63) % 64, self.head)
        self.after = ((ctx + 1) % 64, self.head)
        self.sibling = self.head + 1 - 2 * (self.head % 2)
        self.across = (self.head + 2) % 4
        self.diagonal = (self.sibling + 2) % 4
        self.to_sibling = (ctx, self.sibling)
        self.to_across = (ctx, self.across)
        self.first = ctx == 0
        self.last = ctx // 63
        self.keep, self.send, self.mine = [], [], []
        self.fan_rows, self.fan_peers = [], []
        for colour in range(COLOURS):
            keeps, sends, off = [], [], 0
            for step in range(2):
                length = 256 >> step
                key = self.key[ORDER[colour][step]]
                keeps.append(pl.multiple_of(off + key * length, 32))
                sends.append(pl.multiple_of(off + (1 - key) * length, 32))
                off = off + key * length
            self.keep.append(keeps)
            self.send.append(sends)
            turn = self.y if colour < 2 else self.x
            self.mine.append(pl.multiple_of(off + turn * 32, 32))
            self.fan_rows.append([pl.multiple_of(off + (turn + d) % 4 * 32, 32) for d in (1, 2, 3)])
            self.fan_peers.append(self.along_y if colour < 2 else self.along_x)

    def at(self, x, z, y):
        return (x * 16 + z * 4 + y, self.head)

    def rows_of(self, colour):
        row = 0
        for which in range(COLOURS):
            row = row + jnp.where(colour == which, self.mine[which], 0)
        return pl.multiple_of(row, 32)


def remote(src, dst, send_sem, recv_sem, other):
    return pltpu.make_async_remote_copy(
        src_ref=src, dst_ref=dst, send_sem=send_sem, recv_sem=recv_sem, device_id=other, device_id_type=MESH
    )


def block_of(ref, matrix, row, length, colour):
    if isinstance(colour, int):
        lanes = pl.ds(colour * LANES, LANES)
    else:
        lanes = pl.ds(pl.multiple_of(colour * LANES, LANES), LANES)
    return ref.at[matrix, pl.ds(row, length), lanes]


def mm(a, b):
    return lax.dot_general(a, b, (((1,), (0,)), ((), ())), preferred_element_type=F32)


def mm_nt(a, b):
    return lax.dot_general(a, b, (((1,), (1,)), ((), ())), preferred_element_type=F32)


def mm_tn(a, b):
    return lax.dot_general(a, b, (((0,), (0,)), ((), ())), preferred_element_type=F32)


def square_sum(value):
    rows = jnp.sum(value * value, axis=0, keepdims=True)
    return jnp.sum(rows, axis=1, keepdims=True)


def layer_kernel(
    hidden_hbm, proj_hbm, wout_hbm, up_hbm, down_hbm, rates,
    out_hbm, up_out, down_out, factor_out,
    proj, hidden, wout, state, q_land, o_out, o_land, stat_out, stat_land, attended, mixed, grad, total, moved0, moved1,
    land0, land1, fan_land, z_land, piece, hid, gate_g, up_g, out_g, out_stage, out_acc,
    load_sem, store_sem, q_send, q_recv, o_send, o_recv, st_send, st_recv, h_send, h_recv,
    s_send, s_recv, z_send, z_recv, g_send, g_recv, zg_send, zg_recv, fan_send, fan_recv, fg_send, fg_recv,
):
    place = Place()
    lands = (land0, land1)
    moved = (moved0, moved1)

    loads = [
        pltpu.make_async_copy(proj_hbm.at[1, 0], proj.at[1, 0], load_sem.at[0]),
        pltpu.make_async_copy(proj_hbm.at[2, 0], proj.at[2, 0], load_sem.at[1]),
        pltpu.make_async_copy(up_hbm.at[0, 0], state.at[0], load_sem.at[2]),
        pltpu.make_async_copy(up_hbm.at[1, 0], state.at[1], load_sem.at[3]),
        pltpu.make_async_copy(down_hbm.at[0], state.at[2], load_sem.at[4]),
        pltpu.make_async_copy(proj_hbm.at[0], proj.at[0], load_sem.at[5]),
        pltpu.make_async_copy(proj_hbm.at[1, 1], proj.at[1, 1], load_sem.at[6]),
        pltpu.make_async_copy(proj_hbm.at[2, 1], proj.at[2, 1], load_sem.at[7]),
        pltpu.make_async_copy(wout_hbm, wout, load_sem.at[8]),
        pltpu.make_async_copy(hidden_hbm, hidden, load_sem.at[9]),
    ]
    for load in loads:
        load.start()

    barrier = pltpu.get_barrier_semaphore()
    others = place.along_x + place.along_y + place.z_peer
    others += [place.before, place.after, place.to_sibling, place.to_across]
    for other in others:
        pl.semaphore_signal(barrier, inc=1, device_id=other, device_id_type=MESH)
    pl.semaphore_wait(barrier, len(others))

    def q_copy(block, head, tile):
        lanes, rows = pl.ds(head * HD, HD), pl.ds(tile * HD, HD)
        sem = (block * HEADS + head) * 4 + tile
        return remote(
            proj_hbm.at[0, block, rows, lanes], q_land.at[block, rows, lanes], q_send.at[sem], q_recv.at[sem], place.before
        )

    def o_copy(block, head, tile):
        lanes, rows = pl.ds(head * HD, HD), pl.ds(tile * HD, HD)
        sem = (block * HEADS + head) * 4 + tile
        return remote(
            o_out.at[block, rows, lanes], o_land.at[block, rows, lanes], o_send.at[sem], o_recv.at[sem], place.after
        )

    def stat_copy(block):
        return remote(stat_out.at[block], stat_land.at[block], st_send.at[block], st_recv.at[block], place.after)

    def head_copy(block, kind):
        owner, to = (
            (place.head, place.to_sibling),
            (place.head, place.to_across),
            (place.across, place.to_sibling),
        )[kind]
        rows = mixed.at[owner, block]
        return remote(rows, rows, h_send.at[block, kind], h_recv.at[block, kind], to)

    def scatter_copy(step, matrix, colour):
        length = 256 >> step
        return remote(
            block_of(grad, matrix, place.send[colour][step], length, colour),
            lands[step].at[matrix, colour],
            s_send.at[step, matrix, colour],
            s_recv.at[step, matrix, colour],
            place.partner[ORDER[colour][step]],
        )

    def fan_copy(matrix, colour, d):
        return remote(
            block_of(grad, matrix, place.fan_rows[colour][d], 32, colour),
            fan_land.at[d, matrix, colour],
            fan_send.at[d, matrix, colour],
            fan_recv.at[d, matrix, colour],
            place.fan_peers[colour][d],
        )

    def fan_gather(block, matrix, colour, d):
        own = block_of(moved[block], matrix, place.mine[colour], 32, colour)
        return remote(
            own, own, fg_send.at[d, matrix, colour], fg_recv.at[d, matrix, colour], place.fan_peers[colour][d]
        )

    def z_copy(d, matrix):
        to = place.z_to[d]
        return remote(
            block_of(grad, matrix, place.rows_of(to), 32, to),
            z_land.at[d, matrix],
            z_send.at[d, matrix],
            z_recv.at[d, matrix],
            place.z_peer[d],
        )

    own_row = place.rows_of(place.z)

    def zg_copy(block, d, matrix):
        own = block_of(moved[block], matrix, own_row, 32, place.z)
        return remote(own, own, zg_send.at[d, matrix], zg_recv.at[d, matrix], place.z_peer[d])

    def gather_copy(block, step, matrix, colour):
        kept = block_of(moved[block], matrix, place.keep[colour][step], 256 >> step, colour)
        return remote(
            kept,
            kept,
            g_send.at[step, matrix, colour],
            g_recv.at[step, matrix, colour],
            place.partner[ORDER[colour][step]],
        )

    q_copy(0, 0, 0).start()
    q_copy(0, 0, 1).start()
    q_copy(0, 0, 2).start()
    q_copy(0, 0, 3).start()
    q_copy(0, 1, 0).start()
    q_copy(0, 1, 1).start()
    q_copy(0, 1, 2).start()
    q_copy(0, 1, 3).start()

    def key_pass(block, weights, factors):
        step_scale = -1.0 / math.sqrt(BLOCK_LEN)

        def grown(value, which):
            return value if factors is None else value * factors[which]

        rows_per = 256
        for part in range(TOK // rows_per):
            rows = pl.ds(part * rows_per, rows_per)
            key = proj[1, block, rows, :]
            rate = rates[0, block : block + 1, part * rows_per : (part + 1) * rows_per] * step_scale
            rate = jnp.broadcast_to(rate, (LANES, rows_per)).T
            value = proj[2, block, rows, :].astype(F32)
            out_grad = (value * jnp.concatenate([rate] * 4, axis=1)).astype(BF16)
            out_g[rows, :] = out_grad
            gate = grown(mm(key, weights[0]), 0)
            up = grown(mm(key, weights[1]), 1)
            back = grown(mm_nt(out_grad, weights[2]), 2)
            sig = jax.nn.sigmoid(gate)
            gate_sig = gate * sig
            hid[rows, :] = (gate_sig * up).astype(BF16)
            gate_g[rows, :] = (back * up * (sig + gate_sig * (1.0 - sig))).astype(BF16)
            up_g[rows, :] = (back * gate_sig).astype(BF16)
        for matrix in (2, 1, 0):
            if matrix == 2:
                sums = mm_tn(hid[...], out_g[...])
            elif matrix == 1:
                sums = mm_tn(proj[1, block], up_g[...])
            else:
                sums = mm_tn(proj[1, block], gate_g[...])
            total[matrix] = sums
            grad[matrix] = sums.astype(BF16)
            for colour in range(COLOURS):
                scatter_copy(0, matrix, colour).start()

    def reduction(block, old_factors):
        for step in range(2):
            length = 256 >> step
            for matrix in (2, 1, 0):
                for colour in range(COLOURS):
                    scatter_copy(step, matrix, colour).wait_recv()
                    row = place.keep[colour][step]
                    kept = block_of(total, matrix, row, length, colour)
                    value = kept[...] + lands[step][matrix, colour].astype(F32)
                    kept[...] = value
                    block_of(grad, matrix, row, length, colour)[...] = value.astype(BF16)
                    if step == 0:
                        scatter_copy(1, matrix, colour).start()
                    else:
                        for d in (1, 0, 2):
                            fan_copy(matrix, colour, d).start()
                yield
        for matrix in (2, 1, 0):
            for colour in range(COLOURS):
                kept = block_of(total, matrix, place.mine[colour], 32, colour)
                value = kept[...]
                for d in range(3):
                    fan_copy(matrix, colour, d).wait_recv()
                    value = value + fan_land[d, matrix, colour].astype(F32)
                kept[...] = value
                block_of(grad, matrix, place.mine[colour], 32, colour)[...] = value.astype(BF16)
            for d in range(3):
                z_copy(d, matrix).start()
            yield
        for matrix in (2, 1, 0):
            value = block_of(total, matrix, own_row, 32, place.z)[...]
            for d in range(3):
                z_copy(d, matrix).wait_recv()
                value = value + z_land[d, matrix].astype(F32)
            if block == 0:
                value = block_of(state, matrix, own_row, 32, place.z)[...].astype(F32) - value
                piece[matrix] = value
            else:
                value = piece[matrix] * old_factors[matrix] - value
            block_of(moved[block], matrix, own_row, 32, place.z)[...] = value.astype(BF16)
            for d in range(3):
                zg_copy(block, d, matrix).start()
            yield
        for matrix in (2, 1, 0):
            for d in range(3):
                zg_copy(block, d, matrix).wait_recv()
            for d in (1, 0, 2):
                for colour in range(COLOURS):
                    fan_gather(block, matrix, colour, d).start()
            yield
        for step in (1, 0):
            for matrix in (2, 1, 0):
                for colour in range(COLOURS):
                    if step == 1:
                        for d in range(3):
                            fan_gather(block, matrix, colour, d).wait_recv()
                    else:
                        gather_copy(block, 1, matrix, colour).wait_recv()
                    gather_copy(block, step, matrix, colour).start()
                yield
        for matrix in (2, 1, 0):
            for colour in range(COLOURS):
                gather_copy(block, 0, matrix, colour).wait_recv()
        for matrix in range(3):
            for colour in range(COLOURS):
                for step in range(2):
                    scatter_copy(step, matrix, colour).wait_send()
                    gather_copy(block, step, matrix, colour).wait_send()
                for d in range(3):
                    fan_copy(matrix, colour, d).wait_send()
                    fan_gather(block, matrix, colour, d).wait_send()
            for d in range(3):
                z_copy(d, matrix).wait_send()
                zg_copy(block, d, matrix).wait_send()

    tile_row = lax.broadcasted_iota(jnp.int32, (HD, HD), 0)
    tile_col = lax.broadcasted_iota(jnp.int32, (HD, HD), 1)

    def softmax_part(scores, values):
        peak = jnp.max(scores, axis=1, keepdims=True)
        lifted = jnp.exp2((scores - peak) * SCALE)
        weight = jnp.sum(lifted, axis=1, keepdims=True)
        return mm(lifted.astype(BF16), values), peak * SCALE, weight

    def masked(scores, keep, last):
        width = scores.shape[1]
        if width == HD:
            return jnp.where(keep, scores, -1e30)
        if last:
            return jnp.concatenate([scores[:, : width - HD], jnp.where(keep, scores[:, width - HD :], -1e30)], axis=1)
        return jnp.concatenate([jnp.where(keep, scores[:, :HD], -1e30), scores[:, HD:]], axis=1)

    def far_tile(block, head, tile):
        lanes = pl.ds(head * HD, HD)
        q_copy(block, head, tile).wait_recv()
        source = jnp.maximum(block - place.last, 0)
        rows = pl.ds(tile * HD, HD)
        span = pl.ds(tile * HD, TOK - tile * HD)
        scores = mm_nt(q_land[block, rows, lanes], proj[1, source, span, lanes])
        scores = masked(scores, tile_col > tile_row, False)
        result, peak, weight = softmax_part(scores, proj[2, source, span, lanes])
        o_out[block, rows, lanes] = (result / weight).astype(BF16)
        log_sum = jnp.broadcast_to(peak + jnp.log2(weight), (HD, LANES)).T
        stat_out[block, head : head + 1, rows] = log_sum[:1]
        o_copy(block, head, tile).start()
        if head == HEADS - 1 and tile == 3:
            stat_copy(block).start()

    def near_item(block, head):
        lanes = pl.ds(head * HD, HD)
        for tile in range(4):
            o_copy(block, head, tile).wait_recv()
        if head == 0:
            stat_copy(block).wait_recv()
        for tile in range(4):
            rows = pl.ds(tile * HD, HD)
            span = pl.ds(0, (tile + 1) * HD)
            scores = mm_nt(proj[0, block, rows, lanes], proj[1, block, span, lanes])
            scores = masked(scores, tile_col <= tile_row, True)
            result, peak, weight = softmax_part(scores, proj[2, block, span, lanes])
            far_log = jnp.broadcast_to(stat_land[block, head : head + 1, rows], (LANES, HD)).T
            if block == 0:
                far_log = jnp.where(place.first, -1e30, far_log)
            top = jnp.maximum(peak, far_log)
            near_w = jnp.exp2(peak - top)
            far_w = jnp.exp2(far_log - top)
            far = o_land[block, rows, lanes].astype(F32)
            merged = (result * near_w + far * far_w) / (weight * near_w + far_w)
            attended[block, rows, lanes] = merged.astype(BF16)

    def query_part(block, weights, factors, part):
        rows = pl.ds(part * 256, 256)
        query = proj[0, block, rows, :]
        gate = mm(query, weights[0])
        up = mm(query, weights[1])
        if factors is not None:
            gate = gate * factors[0]
            up = up * factors[1]
        hidden_q = (gate * jax.nn.sigmoid(gate) * up).astype(BF16)
        result = mm(hidden_q, weights[2])
        if factors is not None:
            result = result * factors[2]
        fast = result * lax.rsqrt(jnp.mean(result * result, axis=1, keepdims=True) + 1e-05)
        mixed[place.head, block, rows, :] = (attended[block, rows, :].astype(F32) + fast).astype(BF16)

    def share(block):
        head_copy(block, 0).start()
        head_copy(block, 1).start()

    def forward(block):
        head_copy(block, 1).wait_recv()
        head_copy(block, 2).start()

    def project(block, turn):
        owner = (place.head, place.across, place.sibling, place.diagonal)[turn]
        if turn == 2:
            head_copy(block, 0).wait_recv()
        if turn == 3:
            head_copy(block, 2).wait_recv()
        product = mm(mixed[owner, block], wout[pl.ds(pl.multiple_of(owner * FD, FD), FD), :])
        if turn == 0:
            out_acc[...] = hidden[block].astype(F32) + product
        elif turn < 3:
            out_acc[...] += product
        else:
            out_stage[block] = (out_acc[...] + product).astype(BF16)
            pltpu.make_async_copy(out_stage.at[block], out_hbm.at[block], store_sem.at[block]).start()

    def run(steps, fillers):
        fillers = list(fillers)
        for count, _ in enumerate(steps):
            while fillers and fillers[0][0] <= count:
                fillers.pop(0)[1]()
        for _, filler in fillers:
            filler()

    for load in loads[:5]:
        load.wait()
    key_pass(0, [state[0], state[1], state[2]], None)
    for load in loads[5:]:
        load.wait()
    fillers = [
        (0, lambda: far_tile(0, 0, 0)),
        (0, lambda: far_tile(0, 0, 1)),
        (0, lambda: far_tile(0, 0, 2)),
        (0, lambda: far_tile(0, 0, 3)),
        (0, lambda: far_tile(0, 1, 0)),
        (0, lambda: q_copy(0, 2, 0).start()),
        (1, lambda: far_tile(0, 1, 1)),
        (1, lambda: q_copy(0, 2, 1).start()),
        (2, lambda: far_tile(0, 1, 2)),
        (2, lambda: q_copy(0, 2, 2).start()),
        (3, lambda: far_tile(0, 1, 3)),
        (3, lambda: q_copy(0, 2, 3).start()),
        (4, lambda: far_tile(0, 2, 0)),
        (4, lambda: q_copy(0, 3, 0).start()),
        (5, lambda: far_tile(0, 2, 1)),
        (5, lambda: q_copy(0, 3, 1).start()),
        (6, lambda: far_tile(0, 2, 2)),
        (6, lambda: q_copy(0, 3, 2).start()),
        (7, lambda: far_tile(0, 2, 3)),
        (7, lambda: q_copy(0, 3, 3).start()),
        (8, lambda: far_tile(0, 3, 0)),
        (8, lambda: q_copy(1, 0, 0).start()),
        (9, lambda: far_tile(0, 3, 1)),
        (9, lambda: q_copy(1, 0, 1).start()),
        (10, lambda: far_tile(0, 3, 2)),
        (10, lambda: q_copy(1, 0, 2).start()),
        (11, lambda: far_tile(0, 3, 3)),
        (11, lambda: q_copy(1, 0, 3).start()),
        (12, lambda: far_tile(1, 0, 0)),
        (12, lambda: q_copy(1, 1, 0).start()),
        (13, lambda: far_tile(1, 0, 1)),
        (13, lambda: q_copy(1, 1, 1).start()),
        (14, lambda: far_tile(1, 0, 2)),
        (14, lambda: q_copy(1, 1, 2).start()),
        (15, lambda: far_tile(1, 0, 3)),
        (15, lambda: q_copy(1, 1, 3).start()),
        (16, lambda: far_tile(1, 1, 0)),
        (16, lambda: q_copy(1, 2, 0).start()),
        (17, lambda: far_tile(1, 1, 1)),
        (17, lambda: q_copy(1, 2, 1).start()),
        (18, lambda: far_tile(1, 1, 2)),
        (18, lambda: q_copy(1, 2, 2).start()),
        (19, lambda: far_tile(1, 1, 3)),
        (19, lambda: q_copy(1, 2, 3).start()),
        (20, lambda: far_tile(1, 2, 0)),
        (20, lambda: q_copy(1, 3, 0).start()),
    ]
    run(reduction(0, None), fillers)

    norm = []
    factors = []
    for matrix in range(3):
        first = jnp.sqrt(square_sum(state[matrix].astype(F32)))
        second = square_sum(moved0[matrix].astype(F32))
        factors.append(first * lax.rsqrt(second + 1e-06))
        norm.append(jnp.sqrt(second) * factors[matrix])
    key_pass(1, [moved0[0], moved0[1], moved0[2]], factors)
    fillers = [
        (0, lambda: far_tile(1, 2, 1)),
        (0, lambda: q_copy(1, 3, 1).start()),
        (1, lambda: far_tile(1, 2, 2)),
        (1, lambda: q_copy(1, 3, 2).start()),
        (2, lambda: far_tile(1, 2, 3)),
        (2, lambda: q_copy(1, 3, 3).start()),
        (3, lambda: far_tile(1, 3, 0)),
        (4, lambda: far_tile(1, 3, 1)),
        (4, lambda: near_item(0, 0)),
        (4, lambda: near_item(0, 1)),
        (5, lambda: far_tile(1, 3, 2)),
        (5, lambda: near_item(0, 2)),
        (5, lambda: near_item(0, 3)),
        (6, lambda: far_tile(1, 3, 3)),
        (6, lambda: query_part(0, [state[0], state[1], state[2]], None, 0)),
        (7, lambda: query_part(0, [state[0], state[1], state[2]], None, 1)),
        (7, lambda: share(0)),
        (8, lambda: near_item(1, 0)),
        (8, lambda: near_item(1, 1)),
        (9, lambda: near_item(1, 2)),
        (9, lambda: near_item(1, 3)),
        (10, lambda: query_part(1, [moved0[0], moved0[1], moved0[2]], factors, 0)),
        (11, lambda: query_part(1, [moved0[0], moved0[1], moved0[2]], factors, 1)),
        (11, lambda: share(1)),
        (11, lambda: forward(0)),
        (11, lambda: project(0, 0)),
        (12, lambda: project(0, 1)),
        (12, lambda: project(0, 2)),
        (13, lambda: project(0, 3)),
        (14, lambda: forward(1)),
        (14, lambda: project(1, 0)),
        (14, lambda: project(1, 1)),
        (15, lambda: project(1, 2)),
        (15, lambda: project(1, 3)),
    ]
    run(reduction(1, factors), fillers)

    finals = [
        pltpu.make_async_copy(moved1.at[0], up_out.at[0, 0], store_sem.at[2]),
        pltpu.make_async_copy(moved1.at[1], up_out.at[1, 0], store_sem.at[3]),
        pltpu.make_async_copy(moved1.at[2], down_out.at[0], store_sem.at[4]),
    ]
    for final in finals:
        final.start()
    for matrix in range(3):
        last = square_sum(moved1[matrix].astype(F32))
        factor = norm[matrix] * lax.rsqrt(last + 1e-06)
        factor_out[matrix] = jnp.broadcast_to(factor, (8, LANES))
    for block in range(BLOCKS):
        for head in range(HEADS):
            for tile in range(4):
                q_copy(block, head, tile).wait_send()
                o_copy(block, head, tile).wait_send()
        stat_copy(block).wait_send()
        for kind in range(3):
            head_copy(block, kind).wait_send()
        pltpu.make_async_copy(out_stage.at[block], out_hbm.at[block], store_sem.at[block]).wait()
    for final in finals:
        final.wait()


def body(hidden_in, projected, w_out, fast_up, fast_down, learn_rates):
    dma = pltpu.SemaphoreType.DMA
    vmem = pltpu.VMEM
    hbm_spec = pl.BlockSpec(memory_space=pl.ANY)
    vmem_spec = pl.BlockSpec(memory_space=pltpu.VMEM)
    square = (FD, FD)
    layer_out, up_moved, down_moved, factor = pl.pallas_call(
        layer_kernel,
        out_shape=(
            jax.ShapeDtypeStruct((BLOCKS, TOK, FD), BF16),
            jax.ShapeDtypeStruct((2, 1, FD, FD), BF16),
            jax.ShapeDtypeStruct((1, FD, FD), BF16),
            jax.ShapeDtypeStruct((3, 8, LANES), F32),
        ),
        in_specs=[hbm_spec] * 5 + [vmem_spec],
        out_specs=(hbm_spec, hbm_spec, hbm_spec, vmem_spec),
        scratch_shapes=[
            vmem((3, BLOCKS, TOK, FD), BF16),
            vmem((BLOCKS, TOK, FD), BF16),
            vmem((4 * FD, FD), BF16),
            vmem((3,) + square, BF16),
            vmem((BLOCKS, TOK, FD), BF16),
            vmem((BLOCKS, TOK, FD), BF16),
            vmem((BLOCKS, TOK, FD), BF16),
            vmem((BLOCKS, 8, TOK), F32),
            vmem((BLOCKS, 8, TOK), F32),
            vmem((BLOCKS, TOK, FD), BF16),
            vmem((4, BLOCKS, TOK, FD), BF16),
            vmem((3,) + square, BF16),
            vmem((3,) + square, F32),
            vmem((3,) + square, BF16),
            vmem((3,) + square, BF16),
            vmem((3, COLOURS, 256, LANES), BF16),
            vmem((3, COLOURS, 128, LANES), BF16),
            vmem((3, 3, COLOURS, 32, LANES), BF16),
            vmem((3, 3, 32, LANES), BF16),
            vmem((3, 32, LANES), F32),
            vmem(square, BF16),
            vmem(square, BF16),
            vmem(square, BF16),
            vmem(square, BF16),
            vmem((BLOCKS, TOK, FD), BF16),
            vmem(square, F32),
            dma((10,)),
            dma((5,)),
            dma((32,)),
            dma((32,)),
            dma((32,)),
            dma((32,)),
            dma((2,)),
            dma((2,)),
            dma((2, 3)),
            dma((2, 3)),
            dma((2, 3, COLOURS)),
            dma((2, 3, COLOURS)),
            dma((3, 3)),
            dma((3, 3)),
            dma((2, 3, COLOURS)),
            dma((2, 3, COLOURS)),
            dma((3, 3)),
            dma((3, 3)),
            dma((3, 3, COLOURS)),
            dma((3, 3, COLOURS)),
            dma((3, 3, COLOURS)),
            dma((3, 3, COLOURS)),
        ],
        compiler_params=pltpu.CompilerParams(
            collective_id=0, has_side_effects=True, vmem_limit_bytes=60 << 20
        ),
    )(hidden_in, projected, w_out, fast_up, fast_down, learn_rates)
    return (
        layer_out,
        up_moved.astype(F32) * factor[:2, None, :1, :1],
        down_moved.astype(F32) * factor[2:, :1, :1],
    )


def solution(mesh):
    in_specs = (
        P(None, "ctx", "head"),
        P(None, None, "ctx", "head"),
        P(None, "head"),
        P(None, "head", None, None),
        P("head", None, None),
        P("head", None, "ctx"),
    )
    out_specs = (P(None, "ctx", "head"), P(None, "head", None, None), P("head", None, None))
    return jax.shard_map(body, mesh=mesh, in_specs=in_specs, out_specs=out_specs, check_vma=False)
```
